256 devices in a mesh: fsdp: 8 (over x_hi, y), ctx: 32 (over z, x_lo, core).
Axes of the slice: x: 4 (x_hi: 2, x_lo: 2; x = x_hi * 2 + x_lo), y: 4, z: 8, core: 2. Of those that a mesh axis runs over, the one named last changes fastest.
Arguments:
- tokens: bfloat16 [8, 4096, 1024], P('fsdp', 'ctx'), may hold values from -16 to 16
- cotangent: bfloat16 [8, 4096, 1024], P('fsdp', 'ctx'), may hold values from -6 to 6
- w_query: bfloat16 [1024, 512], P('fsdp')
- w_key: bfloat16 [1024, 512], P('fsdp')
- w_value: bfloat16 [1024, 512], P('fsdp'), may hold values from -0.1875 to 0.1875
- w_out: bfloat16 [512, 1024], P('fsdp'), may hold values from -0.25 to 0.25
- block_mask: int32 [32, 32], replicated, may hold values from 0 to 1, as said below
- span_order: int32 [64], replicated, may hold values from 0 to 63, each once
Outputs:
- mixed_out: bfloat16 [8, 4096, 1024], P('fsdp', 'ctx')
- token_grad: bfloat16 [8, 4096, 1024], P('fsdp', 'ctx')
- grad_query: float32 [1024, 512], P(('fsdp', 'ctx'))
- grad_key: float32 [1024, 512], P(('fsdp', 'ctx'))
- grad_value: float32 [1024, 512], P(('fsdp', 'ctx'))
- grad_out: float32 [512, 1024], P(('fsdp', 'ctx'))
The draws below stay inside these ranges and needn't reach their ends.
Inputs may be any that keep to these rules, and one draw needn't show every extreme that they name: `block_mask`: every diagonal entry is 1.
All inputs are finite; a program needn't handle non-finite values.
Results may differ from the reference program's by a relative error of at most 0.013.
The reference program's roundings to bfloat16 on the way (of `attention` and `d_attention`) count: a program that leaves them out, or rounds other values in their place, can miss the bound.
Values may be sent and summed in bfloat16 or wider, within the bound.
No kernel may reach another device: no remote copies, remote signals or barrier semaphores. Data moves between devices by JAX's collectives and lax.ppermute only.
A program may use at most 128 MiB of HBM per device.

```python
from functools import partial
import jax
import jax.numpy as jnp
from jax import lax

D = 1024
HEADS = 4
HD = 128
BLK = 128
SPAN = 64
HQ = 512
SEQ = 4096
NB = 32
NCH = 64
CLIPS = 8


def projection_base(key):
    return jax.random.normal(jax.random.fold_in(key, 101), (D, HQ), jnp.float32) / D ** 0.5


def draw_w_query(key, part):
    return projection_base(key).astype(jnp.bfloat16)


def draw_w_key(key, part):
    others = jax.random.normal(jax.random.fold_in(key, 202), (D, HQ), jnp.float32) / D ** 0.5
    return others.astype(jnp.bfloat16)


def draw_tokens(key, part):
    base = jax.random.normal(jax.random.fold_in(key, 303), (CLIPS, SEQ, D), jnp.float32)
    return jnp.clip(base, -6.0, 6.0).astype(jnp.bfloat16)


def draw_block_mask(key, part):
    bits = jax.random.randint(jax.random.fold_in(key, 405), (NB, NB), 0, 2, dtype=jnp.int32)
    lanes = jnp.arange(NB, dtype=jnp.int32)
    diagonal = (lanes[:, None] == lanes[None, :]).astype(jnp.int32)
    return jnp.maximum(bits, diagonal)


def steps_of(stream_key, shape, shards, least, top_value):
    def one(dim, shards_of):
        heights = jax.random.uniform(jax.random.fold_in(jax.random.fold_in(stream_key, 6), dim), (shards_of,), jnp.float32, least / len(shards), top_value / len(shards))
        return jnp.repeat(jnp.exp(heights), shape[dim] // shards_of).reshape((-1,) + (1,) * (len(shape) - dim - 1))

    factor_of = one(*shards[0])
    for cut in shards[1:]:
        factor_of = factor_of * one(*cut)
    return factor_of


def normal_values(stream_key, extent, scale, limit, shards=(), kind=jnp.bfloat16):
    loudness = steps_of(stream_key, extent, shards, -0.22, 0.18) if shards else 1.0
    values = jax.random.normal(stream_key, extent, jnp.float32) * scale * loudness
    return jnp.minimum(jnp.maximum(values, -limit), limit).astype(kind)


def setup_inputs(seed: int = 0) -> dict:
    key_of = jax.random.split(jax.random.key(seed), 9)
    return {
        "tokens": draw_tokens(jax.random.fold_in(key_of[8], 71), 0),
        "cotangent": normal_values(key_of[1], (CLIPS, SEQ, D), 1.0, 6.0, ((0, 8), (1, 32))),
        "w_query": draw_w_query(jax.random.fold_in(key_of[8], 71), 0),
        "w_key": draw_w_key(jax.random.fold_in(key_of[8], 71), 0),
        "w_value": normal_values(key_of[4], (D, HQ), D ** -0.5, 0.1875, ((0, 8),)),
        "w_out": normal_values(key_of[5], (HQ, D), HQ ** -0.5, 0.25, ((0, 8),)),
        "block_mask": draw_block_mask(jax.random.fold_in(key_of[8], 71), 0),
        "span_order": jax.random.permutation(key_of[7], NCH).astype(jnp.int32),
    }


NEG = -1e+30

def stored_blocks(span_order):
    rows = jnp.arange(SEQ, dtype=jnp.int32)
    first = span_order[rows // SPAN].astype(jnp.int32)
    return (first * SPAN + rows % SPAN) // BLK

def attend(allowed, qf, kf, vf):
    scale = 1.0 / HD ** 0.5
    score = jnp.einsum('qhd,khd->hqk', qf, kf, precision=lax.Precision.HIGHEST) * scale
    score = jnp.where(allowed[None], score, NEG)
    top = lax.stop_gradient(lax.optimization_barrier(jnp.max(score, axis=-1, keepdims=True)))
    prob = jnp.where(allowed[None], jnp.exp(score - top), 0.0)
    prob = prob / lax.optimization_barrier(jnp.sum(prob, axis=-1, keepdims=True))
    return jnp.einsum('hqk,khd->qhd', prob, vf, precision=lax.Precision.HIGHEST)

def one_clip(x, dy, allowed, w_query, w_key, w_value, w_out):
    shape3 = (SEQ, HEADS, HD)
    query = jnp.dot(x, w_query, preferred_element_type=jnp.float32).astype(jnp.bfloat16)
    keys = jnp.dot(x, w_key, preferred_element_type=jnp.float32).astype(jnp.bfloat16)
    values = jnp.dot(x, w_value, preferred_element_type=jnp.float32).astype(jnp.bfloat16)
    qf = query.astype(jnp.float32).reshape(shape3)
    kf = keys.astype(jnp.float32).reshape(shape3)
    vf = values.astype(jnp.float32).reshape(shape3)
    combined, pull = jax.vjp(partial(attend, allowed), qf, kf, vf)
    attention = combined.reshape(SEQ, HQ).astype(jnp.bfloat16)
    mixed = (x.astype(jnp.float32) + jnp.dot(attention, w_out, preferred_element_type=jnp.float32)).astype(jnp.bfloat16)
    d_attention = jnp.dot(dy, w_out.T, preferred_element_type=jnp.float32).astype(jnp.bfloat16)
    d_query, d_key, d_value = pull(d_attention.astype(jnp.float32).reshape(shape3))
    d_query = d_query.reshape(SEQ, HQ).astype(jnp.bfloat16)
    d_key = d_key.reshape(SEQ, HQ).astype(jnp.bfloat16)
    d_value = d_value.reshape(SEQ, HQ).astype(jnp.bfloat16)
    token_grad = (dy.astype(jnp.float32) + jnp.dot(d_query, w_query.T, preferred_element_type=jnp.float32) + jnp.dot(d_key, w_key.T, preferred_element_type=jnp.float32) + jnp.dot(d_value, w_value.T, preferred_element_type=jnp.float32)).astype(jnp.bfloat16)
    grad_query = jnp.dot(x.T, d_query, preferred_element_type=jnp.float32)
    grad_key = jnp.dot(x.T, d_key, preferred_element_type=jnp.float32)
    grad_value = jnp.dot(x.T, d_value, preferred_element_type=jnp.float32)
    grad_out = jnp.dot(attention.T, dy, preferred_element_type=jnp.float32)
    return (mixed, token_grad, grad_query, grad_key, grad_value, grad_out)

def reference(tokens, cotangent, w_query, w_key, w_value, w_out, block_mask, span_order):
    block = stored_blocks(span_order)
    allowed = block_mask[block][:, block] == 1

    def per_clip(item):
        return one_clip(item[0], item[1], allowed, w_query, w_key, w_value, w_out)
    mixed, token_grad, grad_query, grad_key, grad_value, grad_out = lax.map(per_clip, (tokens, cotangent))
    return (mixed, token_grad, lax.optimization_barrier(jnp.sum(grad_query, axis=0)), lax.optimization_barrier(jnp.sum(grad_key, axis=0)), lax.optimization_barrier(jnp.sum(grad_value, axis=0)), lax.optimization_barrier(jnp.sum(grad_out, axis=0)))
```

```python
import math

import jax
import jax.numpy as jnp
from jax import lax
from jax.experimental import pallas as pl
from jax.experimental.pallas import tpu as pltpu
from jax.sharding import Mesh
from jax.sharding import PartitionSpec as P

HEADS = 4
HD = 128
SPAN = 64
NF = 8
NZ = 8
ROWS = 512
SUB = 256
NEG = -1e30
SCALE = 1.0 / math.sqrt(HD)
C2 = SCALE * math.log2(math.e)
VMEM_LIMIT = 40 << 20
BF = jnp.bfloat16
F32 = jnp.float32


def dot(a, b):
    return jnp.dot(a, b, preferred_element_type=F32)


def dot_nt(a, b):
    return lax.dot_general(a, b, (((1,), (1,)), ((), ())), preferred_element_type=F32)


def dot_tn(a, b):
    return lax.dot_general(a, b, (((0,), (0,)), ((), ())), preferred_element_type=F32)


def with_bias(s, bias_ref, first):
    parts = [
        s[t * SPAN : (t + 1) * SPAN, :] + bias_ref[first + t] for t in range(s.shape[0] // SPAN)
    ]
    return jnp.concatenate(parts, axis=0)


def fold(s, op):
    return op(s.reshape(s.shape[0] // 8, 8, s.shape[1]), axis=0)


def forward_kernel(q_ref, g_ref, *refs):
    chunks, (bias_ref, o_ref, stat_ref, s_scr, acc, row) = refs[:NZ], refs[NZ:]
    q_t = q_ref[...].T
    g_t = g_ref[...].T
    acc[...] = jnp.zeros_like(acc)
    row[0] = jnp.full_like(row[0], NEG)
    row[1] = jnp.zeros_like(row[1])
    row[2] = jnp.zeros_like(row[2])
    for d in range(NZ):
        kv = chunks[d]

        def find_top(i, top, kv=kv, d=d):
            at = pl.multiple_of(i * SUB, SUB)
            s = dot(kv[pl.ds(at, SUB), :HD], q_t) * C2
            s = with_bias(s, bias_ref, d * 8 + i * (SUB // SPAN))
            s_scr[pl.ds(at, SUB), :] = s
            return jnp.maximum(top, fold(s, jnp.max))

        top = lax.fori_loop(0, ROWS // SUB, find_top, jnp.full((8, ROWS), NEG, F32))
        old = row[0]
        new = jnp.maximum(old, jnp.max(top, axis=0, keepdims=True))
        fade = jnp.exp2(old - new)
        row[0] = new
        acc[...] = acc[...] * fade[0:1]

        def add_up(i, carry, kv=kv, new=new):
            total, mixed = carry
            at = pl.multiple_of(i * SUB, SUB)
            e = jnp.exp2(s_scr[pl.ds(at, SUB), :] - new[0:1])
            v = kv[pl.ds(at, SUB), HD:]
            dp = dot(v, g_t)
            acc[...] += dot(v.T, e.astype(BF))
            return (total + fold(e, jnp.sum), mixed + fold(e * dp, jnp.sum))

        zero = jnp.zeros((8, ROWS), F32)
        total, mixed = lax.fori_loop(0, ROWS // SUB, add_up, (zero, zero))
        row[1] = row[1] * fade + jnp.sum(total, axis=0, keepdims=True)
        row[2] = row[2] * fade + jnp.sum(mixed, axis=0, keepdims=True)
    share = 1.0 / row[1]
    o_ref[...] = (acc[...] * share[0:1]).T.astype(BF)
    stat_ref[0:1, :] = (row[0] + jnp.log2(row[1]))[0:1]
    stat_ref[1:2, :] = (row[2] * share)[0:1]


def query_kernel(q_ref, g_ref, stat_ref, *refs):
    chunks, (bias_ref, dq_ref, acc) = refs[:NZ], refs[NZ:]
    q_t = q_ref[...].T
    g_t = g_ref[...].T
    lse = stat_ref[0:1, :]
    delta = stat_ref[1:2, :]
    acc[...] = jnp.zeros_like(acc)
    for d in range(NZ):
        kv = chunks[d]

        @pl.loop(0, ROWS // SUB)
        def _(i, kv=kv, d=d):
            at = pl.multiple_of(i * SUB, SUB)
            k = kv[pl.ds(at, SUB), :HD]
            s = with_bias(dot(k, q_t) * C2, bias_ref, d * 8 + i * (SUB // SPAN))
            p = jnp.exp2(s - lse)
            dp = dot(kv[pl.ds(at, SUB), HD:], g_t)
            ds = (p * (dp - delta)).astype(BF)
            acc[...] += dot(k.T, ds)

    dq_ref[...] = (acc[...].T * SCALE).astype(BF)


def key_kernel(kv_ref, stat_ref, *refs):
    chunks, (bias_ref, dk_ref, dv_ref, dk_acc, dv_acc) = refs[:NZ], refs[NZ:]
    dk_acc[...] = jnp.zeros_like(dk_acc)
    dv_acc[...] = jnp.zeros_like(dv_acc)
    for d in range(NZ):
        qg = chunks[d]
        q_t = qg[:, :HD].T
        g_t = qg[:, HD:].T
        lse = stat_ref[d, 0:1, :]
        delta = stat_ref[d, 1:2, :]

        @pl.loop(0, ROWS // SUB)
        def _(i, qg=qg, q_t=q_t, g_t=g_t, lse=lse, delta=delta, d=d):
            at = pl.multiple_of(i * SUB, SUB)
            s = dot(kv_ref[pl.ds(at, SUB), :HD], q_t) * C2
            s = with_bias(s, bias_ref, d * 8 + i * (SUB // SPAN))
            p = jnp.exp2(s - lse)
            dp = dot(kv_ref[pl.ds(at, SUB), HD:], g_t)
            ds = (p * (dp - delta)).astype(BF)
            dk_acc[pl.ds(at, SUB), :] += dot(ds, qg[:, :HD])
            dv_acc[pl.ds(at, SUB), :] += dot(p.astype(BF), qg[:, HD:])

    dk_ref[...] = (dk_acc[...] * SCALE).astype(BF)
    dv_ref[...] = dv_acc[...].astype(BF)


def call(kernel, name, out_shape, scratch, flops, *args):
    many = isinstance(out_shape, tuple)
    vmem = pl.BlockSpec(memory_space=pltpu.VMEM)
    return pl.pallas_call(
        kernel,
        name=name,
        out_shape=out_shape,
        in_specs=[vmem] * len(args),
        out_specs=(vmem,) * len(out_shape) if many else vmem,
        scratch_shapes=scratch,
        compiler_params=pltpu.CompilerParams(vmem_limit_bytes=VMEM_LIMIT),
        cost_estimate=pl.CostEstimate(
            flops=flops, bytes_accessed=4 << 20, transcendentals=ROWS * ROWS * NZ
        ),
    )(*args)


def shift(x, axis, size, by):
    return lax.ppermute(x, axis, [((i + by) % size, i) for i in range(size)])


def ring(x):
    out = [None] * NZ
    out[0] = x
    for r in range(1, NZ // 2 + 1):
        out[r] = shift(out[r - 1], "z", NZ, 1)
        if r < NZ // 2:
            out[-r] = shift(out[(-r + 1) % NZ], "z", NZ, -1)
    return out


def spread(x, axis, size):
    many = jnp.broadcast_to(x[None], (size,) + x.shape)
    return lax.all_to_all(many, axis, split_axis=0, concat_axis=0, tiled=True)


def span_bias(block_mask, span_order, z):
    order = jnp.concatenate([span_order, span_order])
    order = lax.dynamic_slice(order, (z * 8,), (64,)) // 2
    hot = (order[:, None] == jnp.arange(32, dtype=jnp.int32)[None, :]).astype(F32)
    linked = dot(dot(hot, block_mask.astype(F32)), hot.T)
    bias = jnp.where(linked > 0.5, 0.0, NEG).astype(F32)
    own_queries = jnp.repeat(bias[:8].T, SPAN, axis=1)
    by_group = jnp.transpose(bias[:, :8].reshape(8, 8, 8), (0, 2, 1))
    own_keys = jnp.repeat(by_group.reshape(64, 8), SPAN, axis=1)
    return own_queries[:, None, :], own_keys[:, None, :]


def body(tokens, cotangent, w_query, w_key, w_value, w_out, block_mask, span_order):
    x_own = tokens[0]
    dy_own = cotangent[0]
    h = lax.axis_index("h")
    z = lax.axis_index("z")
    bias_q, bias_k = span_bias(block_mask, span_order, z)

    def head(w):
        return lax.dynamic_slice(w, (0, h * HD), (w.shape[0], HD))

    w_mine = jnp.concatenate([head(w_query), head(w_key), head(w_value)], axis=1)
    w_head = spread(w_mine, "f", NF).reshape(1024, 3 * HD)
    x = lax.all_gather(x_own, "h", axis=0, tiled=True)
    dy = lax.all_gather(dy_own, "h", axis=0, tiled=True)
    out_full = lax.all_gather(w_out, "f", axis=0, tiled=True)
    out_head = lax.dynamic_slice(out_full, (h * HD, 0), (HD, 1024))

    kv = dot(x, w_head[:, HD:]).astype(BF)
    q = dot(x, w_head[:, :HD]).astype(BF)
    g = dot_nt(dy, out_head).astype(BF)
    kv_all = ring(kv)
    work = 2 * ROWS * ROWS * NZ * HD
    head_rows = jax.ShapeDtypeStruct((ROWS, HD), BF)
    att, stat = call(
        forward_kernel,
        "attn_forward",
        (head_rows, jax.ShapeDtypeStruct((2, ROWS), F32)),
        [
            pltpu.VMEM((ROWS, ROWS), F32),
            pltpu.VMEM((HD, ROWS), F32),
            pltpu.VMEM((3, 8, ROWS), F32),
        ],
        3 * work,
        q,
        g,
        *kv_all,
        bias_q,
    )
    qg_all = ring(jnp.concatenate([q, g], axis=1))
    stats = spread(stat.reshape(1, 8, 128), "z", NZ).reshape(NZ, 2, ROWS)
    stats = lax.dynamic_slice(jnp.concatenate([stats, stats]), (z, 0, 0), (NZ, 2, ROWS))
    dq = call(
        query_kernel,
        "attn_query_side",
        head_rows,
        [pltpu.VMEM((HD, ROWS), F32)],
        3 * work,
        q,
        g,
        stat,
        *kv_all,
        bias_q,
    )
    dk, dv = call(
        key_kernel,
        "attn_key_side",
        (head_rows, head_rows),
        [pltpu.VMEM((ROWS, HD), F32), pltpu.VMEM((ROWS, HD), F32)],
        4 * work,
        kv,
        stats,
        *qg_all,
        bias_k,
    )

    att_all = lax.all_gather(att[None], "h", axis=0, tiled=True)
    att_own = lax.dynamic_slice(att_all, (0, h * 128, 0), (HEADS, 128, HD))
    att_own = jnp.transpose(att_own, (1, 0, 2)).reshape(128, HEADS * HD)
    mixed = (x_own.astype(F32) + dot(att_own, out_full)).astype(BF)

    w_all = lax.all_gather(w_head[None], "h", axis=0, tiled=True)
    d_head = jnp.concatenate([dq, dk, dv], axis=1)
    d_own = lax.all_to_all(
        d_head.reshape(HEADS, 128, 3 * HD), "h", split_axis=0, concat_axis=0, tiled=True
    )
    token_grad = dy_own.astype(F32)
    for i in range(HEADS):
        token_grad = token_grad + dot_nt(d_own[i], w_all[i])
    token_grad = token_grad.astype(BF)

    grad_head = dot_tn(x, d_head).astype(BF).reshape(64, 16 * 3 * HD)
    rows_of = jnp.transpose(att_all, (1, 0, 2)).reshape(ROWS, HEADS * HD)
    grad_out = dot_tn(rows_of, dy).astype(BF).reshape(64, 4, 2 * 1024)
    grad_out = lax.dynamic_slice(grad_out, (0, h, 0), (64, 1, 2048)).reshape(64, 2048)
    terms = jnp.concatenate([grad_head, grad_out], axis=1).reshape(64, 64, 128)
    terms = lax.all_to_all(terms, ("f", "z"), split_axis=0, concat_axis=0, tiled=True)
    summed = jnp.sum(terms.astype(F32), axis=0)
    grad_o = summed[48:].reshape(2, 1024)
    grads = summed[:48].reshape(HEADS, 4, 3 * HD)
    grads = lax.all_to_all(grads, "h", split_axis=0, concat_axis=0, tiled=True)
    grads = jnp.transpose(grads.reshape(HEADS, 4, 3, HD), (2, 1, 0, 3)).reshape(3, 4, HEADS * HD)
    return (mixed[None], token_grad[None], grads[0], grads[1], grads[2], grad_o)


def solution(mesh):
    fine = Mesh(mesh.devices.reshape(NF, NZ, HEADS), ("f", "z", "h"))
    rows = P("f", ("z", "h"), None)
    split = P(("f", "z", "h"), None)
    return jax.shard_map(
        body,
        mesh=fine,
        in_specs=(rows, rows, P("f", None), P("f", None), P("f", None), P("f", None), P(), P()),
        out_specs=(rows, rows, split, split, split, split),
        check_vma=False,
    )
```

```python
import functools
import math

import jax
import jax.numpy as jnp
from jax import lax
from jax.experimental import pallas as pl
from jax.experimental.pallas import tpu as pltpu
from jax.sharding import Mesh
from jax.sharding import PartitionSpec as P

HEADS = 4
HD = 128
SPAN = 64
NF = 8
NZ = 8
ROWS = 512
NEG = -1e30
SCALE = 1.0 / math.sqrt(HD)
C2 = SCALE * math.log2(math.e)
FLOPS = 8
VMEM_LIMIT = 40 << 20
BF = jnp.bfloat16
F32 = jnp.float32


def dot(a, b):
    return jnp.dot(a, b, preferred_element_type=F32)


def dot_nt(a, b):
    return lax.dot_general(a, b, (((1,), (1,)), ((), ())), preferred_element_type=F32)


def dot_tn(a, b):
    return lax.dot_general(a, b, (((0,), (0,)), ((), ())), preferred_element_type=F32)


def with_bias(s, bias_ref, firsts):
    parts = []
    for t in range(ROWS // SPAN):
        row = jnp.concatenate([bias_ref[first + t] for first in firsts], axis=1)
        parts.append(s[t * SPAN : (t + 1) * SPAN, :] + row)
    return jnp.concatenate(parts, axis=0)


def tiles(s):
    return [s[:, t * HD : (t + 1) * HD] for t in range(s.shape[1] // HD)]


def wide(row, count):
    return jnp.concatenate([row] * (count * (ROWS // HD)), axis=1)


class Staged:
    def __init__(self, chunks, buf, sems, at_once):
        self.buf, self.sems, self.at_once = buf, sems, at_once
        self.turns = len(chunks) // at_once
        self.copies = [
            pltpu.make_async_copy(
                chunk, buf.at[n // at_once, pl.ds(n % at_once * ROWS, ROWS)], sems.at[n]
            )
            for n, chunk in enumerate(chunks)
        ]
        for copy in self.copies:
            copy.start()

    def turn(self, n):
        for i in range(self.at_once):
            pltpu.make_async_copy(
                self.buf.at[n, pl.ds(i * ROWS, ROWS)],
                self.buf.at[n, pl.ds(i * ROWS, ROWS)],
                self.sems.at[n * self.at_once + i],
            ).wait()
        return self.buf.at[n]


def forward_kernel(count, at_once, first, last, number_ref, *refs):
    q_ref, refs = refs[0], refs[1:]
    chunks, refs = refs[:count], refs[count:]
    bias_ref, refs = refs[0], refs[1:]
    if not first:
        state_in, refs = refs[0], refs[1:]
    if last:
        g_ref, o_ref, stat_ref, row_ref, state, buf, sems = refs
    else:
        state, buf, sems = refs
    blocks = Staged(chunks, buf, sems, at_once)
    if first:
        state[0] = jnp.full_like(state[0], NEG)
        state[1] = jnp.zeros_like(state[1])
        state[2] = jnp.zeros_like(state[2])
    else:
        state[...] = state_in[...]

    @pl.loop(0, blocks.turns)
    def _(n):
        kv = blocks.turn(n)
        s = dot_nt(q_ref[...], kv[:, :HD]) * C2
        s = with_bias(s, bias_ref, [number_ref[n * at_once + i] * 8 for i in range(at_once)])
        old = state[0]
        top = functools.reduce(jnp.maximum, tiles(s))
        new = jnp.maximum(old, jnp.max(top, axis=1, keepdims=True))
        fade = jnp.exp2(old - new)
        e = jnp.exp2(s - wide(new, at_once))
        state[0] = new
        state[1] = state[1] * fade + sum(tiles(e))
        state[2] = state[2] * fade + dot(e.astype(BF), kv[:, HD:])

    if last:
        total = jnp.sum(state[1], axis=1, keepdims=True)
        combined = state[2] * (1.0 / total)
        o_ref[...] = combined.astype(BF)
        lse = state[0] + jnp.log2(total)
        delta = jnp.sum(combined * g_ref[...].astype(F32), axis=1, keepdims=True)
        delta = jnp.broadcast_to(delta, (ROWS, HD))
        row_ref[0] = lse
        row_ref[1] = delta
        stat_ref[0:1, :] = lse.T[0:1, :]
        stat_ref[1:2, :] = delta.T[0:1, :]


def query_kernel(count, at_once, q_ref, g_ref, row_ref, *refs):
    chunks, (bias_ref, dq_ref, acc, buf, sems) = refs[:count], refs[count:]
    blocks = Staged(chunks, buf, sems, at_once)
    acc[...] = jnp.zeros_like(acc)

    @pl.loop(0, blocks.turns)
    def _(n):
        kv = blocks.turn(n)
        s = dot_nt(q_ref[...], kv[:, :HD]) * C2
        s = with_bias(s, bias_ref, [(n * at_once + i) * 8 for i in range(at_once)])
        p = jnp.exp2(s - wide(row_ref[0], at_once))
        dp = dot_nt(g_ref[...], kv[:, HD:])
        ds = (p * (dp - wide(row_ref[1], at_once))).astype(BF)
        acc[...] += dot(ds, kv[:, :HD])

    dq_ref[...] = (acc[...] * SCALE).astype(BF)


def key_kernel(count, at_once, first, last, number_ref, kv_ref, stat_ref, *refs):
    chunks, refs = refs[:count], refs[count:]
    bias_ref, refs = refs[0], refs[1:]
    if not first:
        state_in, refs = refs[0], refs[1:]
    if last:
        d_ref, state, buf, sems = refs
    else:
        state, buf, sems = refs
    blocks = Staged(chunks, buf, sems, at_once)
    if first:
        state[...] = jnp.zeros_like(state)
    else:
        state[...] = state_in[...]

    @pl.loop(0, blocks.turns)
    def _(n):
        qg = blocks.turn(n)
        numbers = [number_ref[n * at_once + i] for i in range(at_once)]
        lse = jnp.concatenate([stat_ref[d, 0:1, :] for d in numbers], axis=1)
        delta = jnp.concatenate([stat_ref[d, 1:2, :] for d in numbers], axis=1)
        s = dot_nt(kv_ref[:, :HD], qg[:, :HD]) * C2
        s = with_bias(s, bias_ref, [d * 8 for d in numbers])
        p = jnp.exp2(s - lse)
        dp = dot_nt(kv_ref[:, HD:], qg[:, HD:])
        ds = (p * (dp - delta)).astype(BF)
        state[0] += dot(ds, qg[:, :HD])
        state[1] += dot(p.astype(BF), qg[:, HD:])

    if last:
        d_ref[:, :HD] = (state[0] * SCALE).astype(BF)
        d_ref[:, HD:] = state[1].astype(BF)


def call(kernel, name, out_shape, scratch, flops, *args):
    many = isinstance(out_shape, tuple)
    vmem = pl.BlockSpec(memory_space=pltpu.VMEM)
    smem = pl.BlockSpec(memory_space=pltpu.SMEM)
    return pl.pallas_call(
        kernel,
        name=name,
        out_shape=out_shape,
        in_specs=[smem if a.dtype == jnp.int32 else vmem for a in args],
        out_specs=(vmem,) * len(out_shape) if many else vmem,
        scratch_shapes=scratch,
        compiler_params=pltpu.CompilerParams(vmem_limit_bytes=VMEM_LIMIT),
        cost_estimate=pl.CostEstimate(
            flops=flops, bytes_accessed=1 << 20, transcendentals=flops // 2560
        ),
    )(*args)


def take(x, axis, size, by):
    return lax.ppermute(x, axis, [((i + by) % size, i) for i in range(size)])


def swap(x, bit):
    return lax.ppermute(x, "h", [(i, i ^ bit) for i in range(HEADS)])


def gather(x):
    far = swap(x, 2)
    return jnp.concatenate([x, swap(x, 1), far, swap(far, 1)], axis=0)


def add_heads(terms):
    blocks = terms.reshape(HEADS, ROWS // HEADS, terms.shape[1])
    near = swap(jnp.stack([blocks[1], blocks[3]]).astype(BF), 1).astype(F32)
    return blocks[0] + near[0] + swap((blocks[2] + near[1]).astype(BF), 2).astype(F32)


def after(x, *others):
    return lax.optimization_barrier((x,) + others)[0]


def exchange(x, axis):
    return lax.all_to_all(x, axis, split_axis=0, concat_axis=0, tiled=True)


def ring(x):
    out = [None] * NZ
    out[0] = x
    for r in range(1, NZ // 2 + 1):
        out[r] = take(out[r - 1], "z", NZ, 1)
        if r < NZ // 2:
            out[-r] = take(out[(-r + 1) % NZ], "z", NZ, -1)
    return out


def spread(x, axis, size):
    return exchange(jnp.broadcast_to(x[None], (size,) + x.shape), axis)


def span_bias(block_mask, span_order, z, h):
    order = jnp.tile(span_order.reshape(NZ, 2, 2, 2), (2, 1, 1, 1))
    order = lax.dynamic_slice(order, (z, 0, 0, 0), (NZ, 2, 2, 2))
    order = jnp.where(h // 2 == 1, order[:, ::-1], order)
    order = jnp.where(h % 2 == 1, order[:, :, ::-1], order).reshape(64) // 2
    hot = (order[:, None] == jnp.arange(32, dtype=jnp.int32)[None, :]).astype(F32)
    linked = dot(dot(hot, block_mask.astype(F32)), hot.T)
    bias = jnp.where(linked > 0.5, 0.0, NEG).astype(F32)
    of_queries = jnp.transpose(bias[:8].reshape(8, NZ, 8), (1, 0, 2)).reshape(64, 8)
    of_keys = jnp.transpose(bias[:, :8].reshape(NZ, 8, 8), (0, 2, 1)).reshape(64, 8)
    both = jnp.repeat(jnp.concatenate([of_queries, of_keys]), SPAN, axis=1)
    return both[:64, None, :], both[64:, None, :]


def body(tokens, cotangent, w_query, w_key, w_value, w_out, block_mask, span_order):
    x_own = tokens[0]
    dy_own = cotangent[0]
    h = lax.axis_index("h")
    z = lax.axis_index("z")
    bias_q, bias_k = span_bias(block_mask, span_order, z, h)

    def head(w):
        return lax.dynamic_slice(w, (0, h * HD), (w.shape[0], HD))

    pairs = [(f * HEADS + i, (4 * (f % 2) + i) * HEADS + f // 2) for f in range(NF) for i in range(HEADS)]
    w_part = lax.ppermute(lax.dynamic_slice(w_out, (h * 16, 0), (16, 1024)), ("f", "h"), pairs)
    x = gather(x_own)
    mine = [head(w_key), head(w_value), head(w_query), w_part.reshape(HD, HD)]
    w_got = spread(jnp.concatenate(mine, axis=1), "f", NF).reshape(1024, 4 * HD)
    w_head = w_got[:, : 3 * HD]

    kv = dot(x, w_head[:, : 2 * HD]).astype(BF)
    q = dot(x, w_head[:, 2 * HD :]).astype(BF)
    kv_all = ring(kv)

    dy = gather(after(dy_own, x))
    out_head = w_got[:, 3 * HD :].reshape(HD, 1024)
    g = dot_nt(dy, out_head).astype(BF)
    qg_all = ring(jnp.concatenate([q, g], axis=1))

    work = FLOPS * ROWS * ROWS * HD
    head_rows = jax.ShapeDtypeStruct((ROWS, HD), BF)
    state_shape = (3, ROWS, HD)

    def staging(count, at_once):
        blocks = pltpu.VMEM((count // at_once, at_once * ROWS, 2 * HD), BF)
        return [blocks, pltpu.SemaphoreType.DMA((count,))]

    state = ()
    for number in ((0,), (1, 7), (2, 6), (3, 5)):
        count = len(number)
        state = (
            call(
                functools.partial(forward_kernel, count, count, not state, False),
                "attn_forward",
                jax.ShapeDtypeStruct(state_shape, F32),
                staging(count, count),
                2 * work * count,
                jnp.array(number, jnp.int32),
                q,
                *[kv_all[d] for d in number],
                bias_q,
                *state,
            ),
        )
    att, stat, row = call(
        functools.partial(forward_kernel, 1, 1, False, True),
        "attn_forward_end",
        (
            head_rows,
            jax.ShapeDtypeStruct((2, ROWS), F32),
            jax.ShapeDtypeStruct((2, ROWS, HD), F32),
        ),
        [pltpu.VMEM(state_shape, F32)] + staging(1, 1),
        2 * work,
        jnp.array((4,), jnp.int32),
        q,
        kv_all[4],
        bias_q,
        *state,
        g,
    )
    stats = spread(stat.reshape(1, 8, 128), "z", NZ)
    dq = call(
        functools.partial(query_kernel, NZ, 2),
        "attn_query_side",
        head_rows,
        [pltpu.VMEM((ROWS, HD), F32)] + staging(NZ, 2),
        3 * work * NZ,
        q,
        g,
        row,
        *kv_all,
        bias_q,
    )

    mixed = (x_own.astype(F32) + add_heads(dot(att, out_head))).astype(BF)

    def scatter(terms):
        return jnp.sum(exchange(terms, ("f", "z")).astype(F32), axis=0)

    moved = jnp.arange(HD, dtype=jnp.int32).reshape(2, 4, NZ, 2)
    moved = (moved // 64) * 64 + (moved // 2 % 8) * 8 + (moved // 16 % 4) * 2 + moved % 2
    move = (jnp.arange(HD, dtype=jnp.int32)[:, None] == moved.reshape(1, HD)).astype(BF)
    grad_o = dot_tn(dot(att, move).astype(BF), dy).astype(BF)
    early_terms = jnp.concatenate(
        [grad_o.reshape(64, 16, 128), dot_tn(x, dq).astype(BF).reshape(64, 16, HD)], axis=1
    )
    early = scatter(early_terms)

    stats = after(stats, early_terms).reshape(NZ, 2, ROWS)
    stats = lax.dynamic_slice(jnp.concatenate([stats, stats]), (z, 0, 0), (NZ, 2, ROWS))
    acc_shape = (2, ROWS, HD)
    number = (0, 1, 7, 2, 6, 3)
    part = call(
        functools.partial(key_kernel, len(number), 2, True, False),
        "attn_key_side",
        jax.ShapeDtypeStruct(acc_shape, F32),
        staging(len(number), 2),
        4 * work * len(number),
        jnp.array(number, jnp.int32),
        kv,
        stats,
        *[qg_all[d] for d in number],
        bias_k,
    )
    stats = after(stats, early, mixed)
    number = (5, 4)
    dkv = call(
        functools.partial(key_kernel, len(number), 2, False, True),
        "attn_key_side_end",
        jax.ShapeDtypeStruct((ROWS, 2 * HD), BF),
        [pltpu.VMEM(acc_shape, F32)] + staging(len(number), 2),
        4 * work * len(number),
        jnp.array(number, jnp.int32),
        kv,
        stats,
        *[qg_all[d] for d in number],
        bias_k,
        part,
    )
    pairs = [((4 * e + i) * 4 + a, (2 * a + e) * 4 + i) for e in range(2) for i in range(4) for a in range(4)]
    grad_o = lax.ppermute(early[:16], ("f", "h"), pairs).reshape(2, 1024)
    grad_q = early[16:]

    late_terms = dot_tn(x, dkv).astype(BF).reshape(64, 16, 2 * HD)
    late = scatter(late_terms)
    d_head = jnp.concatenate([after(dkv, late_terms), dq], axis=1)
    token_grad = (dy_own.astype(F32) + add_heads(dot_nt(d_head, w_head))).astype(BF)

    grads = jnp.concatenate([grad_q, late], axis=1).reshape(HEADS, 4, 3 * HD)
    grads = exchange(grads, "h").reshape(HEADS, 4, 3, HD)
    grads = jnp.transpose(grads, (2, 1, 0, 3)).reshape(3, 4, HEADS * HD)
    return (mixed[None], token_grad[None], grads[0], grads[1], grads[2], grad_o)


def solution(mesh):
    fine = Mesh(mesh.devices.reshape(NF, NZ, HEADS), ("f", "z", "h"))
    rows = P("f", ("z", "h"), None)
    split = P(("f", "z", "h"), None)
    return jax.shard_map(
        body,
        mesh=fine,
        in_specs=(rows, rows, P("f", None), P("f", None), P("f", None), P("f", None), P(), P()),
        out_specs=(rows, rows, split, split, split, split),
        check_vma=False,
    )
```

```python
import functools
import math

import jax
import jax.numpy as jnp
from jax import lax
from jax.experimental import pallas as pl
from jax.experimental.pallas import tpu as pltpu
from jax.sharding import Mesh
from jax.sharding import PartitionSpec as P

HEADS = 4
HD = 128
SPAN = 64
NF = 8
NZ = 8
ROWS = 512
NEG = -1e30
SCALE = 1.0 / math.sqrt(HD)
C2 = SCALE * math.log2(math.e)
FLOPS = 8
VMEM_LIMIT = 16 << 20
BF = jnp.bfloat16
F32 = jnp.float32


def dot(a, b):
    return jnp.dot(a, b, preferred_element_type=F32)


def dot_nt(a, b):
    return lax.dot_general(a, b, (((1,), (1,)), ((), ())), preferred_element_type=F32)


def dot_tn(a, b):
    return lax.dot_general(a, b, (((0,), (0,)), ((), ())), preferred_element_type=F32)


def with_bias(s, bias_ref, firsts):
    parts = []
    for t in range(ROWS // SPAN):
        row = jnp.concatenate([bias_ref[first + t] for first in firsts], axis=1)
        parts.append(s[t * SPAN : (t + 1) * SPAN, :] + row)
    return jnp.concatenate(parts, axis=0)


def tiles(s):
    return [s[:, t * HD : (t + 1) * HD] for t in range(s.shape[1] // HD)]


def wide(row, count):
    return jnp.concatenate([row] * (count * (ROWS // HD)), axis=1)


class Staged:
    def __init__(self, pieces, buf, sems, at_once):
        self.buf, self.sems = buf, sems
        self.turns, size = buf.shape[0], at_once * ROWS
        self.parts = [[] for _ in range(self.turns)]
        first = 0
        for n, piece in enumerate(pieces):
            turn, row = divmod(first, size)
            self.parts[turn].append((n, row, piece.shape[0]))
            pltpu.make_async_copy(
                piece, buf.at[turn, pl.ds(row, piece.shape[0])], sems.at[n]
            ).start()
            first += piece.shape[0]

    def turn(self, n):
        def wait(parts, number):
            for i, (_, row, rows) in enumerate(parts):
                block = self.buf.at[n, pl.ds(row, rows)]
                pltpu.make_async_copy(block, block, self.sems.at[number + i]).wait()

        usual = len(self.parts[0])
        if len(self.parts[-1]) == usual:
            wait(self.parts[0], n * usual)
        else:

            @pl.when(n < self.turns - 1)
            def _():
                wait(self.parts[0], n * usual)

            @pl.when(n == self.turns - 1)
            def _():
                wait(self.parts[-1], (self.turns - 1) * usual)

        return self.buf.at[n]


def forward_kernel(pieces, at_once, first, last, number_ref, *refs):
    q_ref, refs = refs[0], refs[1:]
    chunks, refs = refs[:pieces], refs[pieces:]
    bias_ref, refs = refs[0], refs[1:]
    if not first:
        state_in, refs = refs[0], refs[1:]
    if last:
        g_ref, o_ref, stat_ref, state, buf, sems = refs
    else:
        state, buf, sems = refs
    blocks = Staged(chunks, buf, sems, at_once)
    if first:
        state[0] = jnp.full_like(state[0], NEG)
        state[1] = jnp.zeros_like(state[1])
        state[2] = jnp.zeros_like(state[2])
    else:
        state[...] = state_in[...]

    @pl.loop(0, blocks.turns)
    def _(n):
        kv = blocks.turn(n)
        s = dot_nt(q_ref[...], kv[:, :HD]) * C2
        s = with_bias(s, bias_ref, [number_ref[n * at_once + i] * 8 for i in range(at_once)])
        old = state[0]
        top = functools.reduce(jnp.maximum, tiles(s))
        new = jnp.maximum(old, jnp.max(top, axis=1, keepdims=True))
        fade = jnp.exp2(old - new)
        e = jnp.exp2(s - wide(new, at_once))
        state[0] = new
        state[1] = state[1] * fade + sum(tiles(e))
        state[2] = state[2] * fade + dot(e.astype(BF), kv[:, HD:])

    if last:
        total = jnp.sum(state[1], axis=1, keepdims=True)
        combined = state[2] * (1.0 / total)
        o_ref[...] = combined.astype(BF)
        lse = state[0] + jnp.log2(total)
        delta = jnp.sum(combined * g_ref[...].astype(F32), axis=1, keepdims=True)
        delta = jnp.broadcast_to(delta, (ROWS, HD))
        stat_ref[0:1, :] = lse.T[0:1, :]
        stat_ref[1:2, :] = delta.T[0:1, :]


def backward_kernel(pieces, count, first, last, q_ref, g_ref, stat_ref, number_ref, *refs):
    chunks, refs = refs[:pieces], refs[pieces:]
    bias_ref, refs = refs[0], refs[1:]
    if not first:
        acc_in, refs = refs[0], refs[1:]
    parts, refs = refs[:count], refs[count:]
    if last:
        dq_ref, acc, buf, sems = refs
    else:
        acc, buf, sems = refs
    kv = Staged(chunks, buf, sems, count).turn(0)
    q = q_ref[...]
    g = g_ref[...]
    k = kv[:, :HD]
    s = dot_nt(k, q) * C2
    rows = []
    for n in range(count):
        for t in range(ROWS // SPAN):
            first_row = n * ROWS + t * SPAN
            rows.append(s[first_row : first_row + SPAN, :] + bias_ref[number_ref[n] * 8 + t])
    p = jnp.exp2(jnp.concatenate(rows, axis=0) - stat_ref[0:1, :])
    dp = dot_nt(kv[:, HD:], g)
    ds = (p * (dp - stat_ref[1:2, :])).astype(BF)
    dk = (dot(ds, q) * SCALE).astype(BF)
    dv = dot(p.astype(BF), g).astype(BF)
    for n, part in enumerate(parts):
        part[:, :HD] = dk[n * ROWS : (n + 1) * ROWS]
        part[:, HD:] = dv[n * ROWS : (n + 1) * ROWS]
    term = dot(k.T, ds)
    acc[...] = term if first else acc_in[...] + term
    if last:
        dq_ref[...] = (acc[...] * SCALE).T.astype(BF)


def tokens_kernel(*refs):
    blocks, (w_ref, kv_ref, q_ref, x_ref) = refs[:HEADS], refs[HEADS:]
    for d, block in enumerate(blocks):
        rows = pl.ds(d * block.shape[0], block.shape[0])
        x_ref[rows, :] = block[...]
        kvq = dot(block[...], w_ref[:, : 3 * HD]).astype(BF)
        kv_ref[rows, :] = kvq[:, : 2 * HD]
        q_ref[rows, :] = kvq[:, 2 * HD :]


def cotangent_kernel(f_ref, a_ref, b_ref, *refs):
    blocks, (g_ref, dy_ref, out_ref) = refs[:HEADS], refs[HEADS:]
    size = a_ref.shape[0]
    turned = f_ref[0] // (NF // 2) * size
    out_ref[pl.ds(pl.multiple_of(turned, size), size), :] = a_ref[...]
    out_ref[pl.ds(pl.multiple_of(size - turned, size), size), :] = b_ref[...]
    for d, block in enumerate(blocks):
        rows = pl.ds(d * block.shape[0], block.shape[0])
        dy_ref[rows, :] = block[...]
        g_ref[rows, :] = dot_nt(block[...], out_ref[...]).astype(BF)


def out_kernel(h_ref, *refs):
    blocks, (dy_ref, o_ref) = refs[:HEADS], refs[HEADS:]
    h = h_ref[0]
    size = ROWS // HEADS
    dy = dy_ref[:, pl.ds(pl.multiple_of(h * 256, 256), 256)]
    for d, block in enumerate(blocks):
        rows = jnp.concatenate(
            [block[(i ^ d) * size : ((i ^ d) + 1) * size, :] for i in range(HEADS)], axis=0
        )
        grad = dot_tn(rows, dy).astype(BF)
        for e in range(2):
            for c in range(2):
                o_ref[2 * (h ^ d) + e, c * 64 : (c + 1) * 64, :] = grad[
                    e * 64 : (e + 1) * 64, c * HD : (c + 1) * HD
                ]


def call(kernel, name, out_shape, scratch, flops, *args, there=()):
    many = isinstance(out_shape, tuple)
    vmem = pl.BlockSpec(memory_space=pltpu.VMEM)
    smem = pl.BlockSpec(memory_space=pltpu.SMEM)
    specs = [smem if a.dtype == jnp.int32 else vmem for a in args]
    for n in there:
        specs[n] = pl.BlockSpec(memory_space=pl.ANY)
    return pl.pallas_call(
        kernel,
        name=name,
        out_shape=out_shape,
        in_specs=specs,
        out_specs=(vmem,) * len(out_shape) if many else vmem,
        scratch_shapes=scratch,
        compiler_params=pltpu.CompilerParams(vmem_limit_bytes=VMEM_LIMIT),
        cost_estimate=pl.CostEstimate(
            flops=flops, bytes_accessed=1 << 20, transcendentals=flops // 2560
        ),
    )(*args)


def take(x, axis, size, by):
    return lax.ppermute(x, axis, [((i + by) % size, i) for i in range(size)])


def swap(x, bit):
    return lax.ppermute(x, "h", [(i, i ^ bit) for i in range(HEADS)])


def gather(x):
    far = swap(x, 2)
    return [x, swap(x, 1), far, swap(far, 1)]


def after(x, *others):
    return lax.optimization_barrier((x,) + others)[0]


def add_sibling(terms):
    blocks = terms.reshape(HEADS, ROWS // HEADS, terms.shape[1])
    near = swap(jnp.stack([blocks[1], blocks[3]]).astype(BF), 1).astype(F32)
    return blocks[0] + near[0], (blocks[2] + near[1]).astype(BF)


def add_neighbour(sums, *others):
    return sums[0] + swap(after(sums[1], *others), 2).astype(F32)


def exchange(x, axis):
    return lax.all_to_all(x, axis, split_axis=0, concat_axis=0, tiled=True)


class Ring:
    def __init__(self, block):
        self.blocks = {0: [block]}
        self.steps = 0

    def step(self, *others):
        r = self.steps = self.steps + 1
        up, down = self.blocks[r - 1][0], self.blocks[(1 - r) % NZ][0]
        if r < NZ // 2:
            self.blocks[r] = [take(after(up, *others), "z", NZ, 1)]
            self.blocks[NZ - r] = [take(after(down, *others), "z", NZ, -1)]
        else:
            half = ROWS // 2
            self.blocks[r] = [
                take(after(up[:half], *others), "z", NZ, 1),
                take(after(down[half:], *others), "z", NZ, -1),
            ]

    def pieces(self, number):
        return [piece for d in number for piece in self.blocks[d]]


def spread(x, axis, size):
    return exchange(jnp.broadcast_to(x[None], (size,) + x.shape), axis)


def span_bias(block_mask, span_order, z, h):
    order = jnp.tile(span_order.reshape(NZ, 2, 2, 2), (2, 1, 1, 1))
    order = lax.dynamic_slice(order, (z, 0, 0, 0), (NZ, 2, 2, 2))
    order = jnp.where(h // 2 == 1, order[:, ::-1], order)
    order = jnp.where(h % 2 == 1, order[:, :, ::-1], order).reshape(64) // 2
    hot = (order[:, None] == jnp.arange(32, dtype=jnp.int32)[None, :]).astype(F32)
    linked = dot(dot(hot, block_mask.astype(F32)), hot.T)
    bias = jnp.where(linked > 0.5, 0.0, NEG).astype(F32)
    by_group = jnp.transpose(bias[:8].reshape(8, NZ, 8), (1, 0, 2)).reshape(64, 8)
    both = jnp.repeat(jnp.concatenate([by_group, bias[:8].T]), SPAN, axis=1)
    return both[:64, None, :], both[64:, None, :]


def body(tokens, cotangent, w_query, w_key, w_value, w_out, block_mask, span_order):
    x_own = tokens[0]
    dy_own = cotangent[0]
    h = lax.axis_index("h")
    z = lax.axis_index("z")
    bias_q, bias_b = span_bias(block_mask, span_order, z, h)

    def head(w):
        return lax.dynamic_slice(w, (0, h * HD), (w.shape[0], HD))

    work = FLOPS * ROWS * ROWS * HD
    head_rows = jax.ShapeDtypeStruct((ROWS, HD), BF)
    pair_rows = jax.ShapeDtypeStruct((ROWS, 2 * HD), BF)
    model_rows = jax.ShapeDtypeStruct((ROWS, 1024), BF)
    state_shape = (3, ROWS, HD)
    acc_shape = (HD, ROWS)

    def staging(groups, at_once, pieces):
        blocks = pltpu.VMEM((groups // at_once, at_once * ROWS, 2 * HD), BF)
        return [blocks, pltpu.SemaphoreType.DMA((pieces,))]

    def half_of_head(turned):
        pairs = []
        for m in range(NF):
            for a in range(HEADS):
                clip = 2 * a + (m // 4) ^ turned
                pairs.append((clip * HEADS + m % 4, m * HEADS + a))
        return lax.ppermute(w_out, ("f", "h"), pairs)

    mine = jnp.concatenate([head(w_key), head(w_value), head(w_query)], axis=1)
    w_head = spread(mine, "f", NF).reshape(1024, 3 * HD)
    kv, q, x = call(
        tokens_kernel,
        "tokens",
        (pair_rows, head_rows, model_rows),
        [],
        3 * work,
        *gather(x_own),
        after(w_head, bias_q, bias_b),
    )
    kv_ring = Ring(kv)
    kv_ring.step()
    g, dy, out_head = call(
        cotangent_kernel,
        "cotangent",
        (head_rows, model_rows, jax.ShapeDtypeStruct((HD, 1024), BF)),
        [],
        2 * work,
        lax.axis_index("f").reshape(1),
        half_of_head(0),
        half_of_head(1),
        *gather(after(dy_own, *kv_ring.blocks[1])),
    )

    def forward(number, state, *more, q=q):
        pieces = kv_ring.pieces(number)
        last = bool(more)
        shape = jax.ShapeDtypeStruct(state_shape, F32)
        if last:
            shape = (
                head_rows,
                jax.ShapeDtypeStruct((2, ROWS), F32),
            )
        count = len(number)
        return call(
            functools.partial(forward_kernel, len(pieces), count, not state, last),
            "attn_forward_end" if last else "attn_forward",
            shape,
            ([pltpu.VMEM(state_shape, F32)] if last else []) + staging(count, count, len(pieces)),
            2 * work * count,
            jnp.array(number, jnp.int32),
            q,
            *pieces,
            bias_q,
            *state,
            *more,
            there=range(2, 2 + len(pieces)),
        )

    kv_ring.step()
    state = (forward((0, 1, 7), ()),)
    kv_ring.step(*state)
    state = (forward((2, 6), state),)
    kv_ring.step(*state)
    state = (forward((3, 5), state),)
    att, stat = forward((4,), state, g)

    def backward(number, acc, last=False):
        pieces = kv_ring.pieces(number)
        count = len(number)
        acc_like = jax.ShapeDtypeStruct(acc_shape, F32)
        out = call(
            functools.partial(backward_kernel, len(pieces), count, not acc, last),
            "attn_backward",
            (pair_rows,) * count + (head_rows if last else acc_like,),
            ([pltpu.VMEM(acc_shape, F32)] if last else []) + staging(count, count, len(pieces)),
            5 * work * count,
            q,
            g,
            stat,
            jnp.array(number, jnp.int32),
            *pieces,
            bias_b,
            *acc,
            there=range(4, 4 + len(pieces)),
        )
        return out[:-1], out[-1]

    def add(part, got):
        return (part.astype(F32) + got.astype(F32)).astype(BF)

    half = ROWS // 2
    (part,), acc = backward((4,), ())
    up = take(part[:half], "z", NZ, -1)
    down = take(part[half:], "z", NZ, 1)
    (part_up, part_down), acc = backward((3, 5), (acc,))
    up = jnp.concatenate([add(part_up[:half], up), part_up[half:]], axis=0)
    down = jnp.concatenate([part_down[:half], add(part_down[half:], down)], axis=0)
    for number in ((2, 6), (1, 7)):
        (part_up, part_down), acc = backward(number, (after(acc, up, down),))
        up, down = take(up, "z", NZ, -1), take(down, "z", NZ, 1)
        up, down = add(part_up, up), add(part_down, down)
    (part,), dq = backward((0,), (after(acc, up, down),), last=True)
    up, down = take(up, "z", NZ, -1), take(down, "z", NZ, 1)

    mixed = add_neighbour(add_sibling(dot(att, out_head)))
    mixed = (x_own.astype(F32) + mixed).astype(BF)
    grad_o = call(
        out_kernel,
        "grad_out",
        jax.ShapeDtypeStruct((NF, HD, HD), BF),
        [],
        2 * work,
        h.reshape(1),
        *gather(att),
        dy,
    )
    grad_q = dot_tn(x, dq).astype(BF).reshape(NF, HD, HD)

    def over_clips(terms):
        return jnp.sum(exchange(terms, "f").astype(F32), axis=0).astype(BF)

    got_qo = over_clips(jnp.concatenate([grad_q, grad_o], axis=2))

    own = after(part, got_qo)
    dkv = (own.astype(F32) + up.astype(F32) + down.astype(F32)).astype(BF)

    terms = dot_tn(x, dkv).astype(BF).reshape(NF, HD, 2 * HD)
    got_kv = over_clips(terms)
    got_o = jnp.transpose(got_qo[:, HD:].reshape(2, 32, 2, HD), (1, 0, 2, 3)).reshape(32, 4, HD)
    got = [got_qo[:, :HD].reshape(32, 4, HD), got_kv.reshape(32, 4, 2 * HD), got_o]
    got = jnp.concatenate(got, axis=2)
    d_head = jnp.concatenate([after(dkv, terms), dq], axis=1)
    token_grad = add_neighbour(add_sibling(dot_nt(d_head, w_head)), got)
    token_grad = (dy_own.astype(F32) + token_grad).astype(BF)

    sums = after(exchange(got, ("z", "h")), token_grad).reshape(NZ, HEADS, 4, 4 * HD)
    sums = jnp.sum(sums.astype(F32), axis=0)
    grads = sums[:, :, : 3 * HD].reshape(HEADS, 4, 3, HD)
    grads = jnp.transpose(grads, (2, 1, 0, 3)).reshape(3, 4, HEADS * HD)
    grad_o = sums[:, :, 3 * HD :].reshape(HEADS, 2, 2, HD)
    grad_o = jnp.transpose(grad_o, (2, 0, 1, 3)).reshape(2, 1024)
    return (mixed[None], token_grad[None], grads[0], grads[1], grads[2], grad_o)


def solution(mesh):
    fine = Mesh(mesh.devices.reshape(NF, NZ, HEADS), ("f", "z", "h"))
    rows = P("f", ("z", "h"), None)
    split = P(("f", "z", "h"), None)
    return jax.shard_map(
        body,
        mesh=fine,
        in_specs=(rows, rows, P("f", None), P("f", None), P("f", None), P("f", None), P(), P()),
        out_specs=(rows, rows, split, split, split, split),
        check_vma=False,
    )
```

```python
import functools
import math

import jax
import jax.numpy as jnp
from jax import lax
from jax.experimental import pallas as pl
from jax.experimental.pallas import tpu as pltpu
from jax.sharding import Mesh
from jax.sharding import PartitionSpec as P

HEADS = 4
HD = 128
SPAN = 64
NF = 8
NZ = 8
ROWS = 512
NEG = -1e30
SCALE = 1.0 / math.sqrt(HD)
C2 = SCALE * math.log2(math.e)
FLOPS = 8
VMEM_LIMIT = 16 << 20
BF = jnp.bfloat16
F32 = jnp.float32


def dot(a, b):
    return jnp.dot(a, b, preferred_element_type=F32)


def dot_nt(a, b):
    return lax.dot_general(a, b, (((1,), (1,)), ((), ())), preferred_element_type=F32)


def dot_tn(a, b):
    return lax.dot_general(a, b, (((0,), (0,)), ((), ())), preferred_element_type=F32)


def with_bias(s, bias_ref, firsts):
    parts = []
    for t in range(ROWS // SPAN):
        row = jnp.concatenate([bias_ref[first + t] for first in firsts], axis=1)
        parts.append(s[t * SPAN : (t + 1) * SPAN, :] + row)
    return jnp.concatenate(parts, axis=0)


def tiles(s):
    return [s[:, t * HD : (t + 1) * HD] for t in range(s.shape[1] // HD)]


def wide(row, count):
    return jnp.concatenate([row] * (count * (ROWS // HD)), axis=1)


class Staged:
    def __init__(self, pieces, buf, sems, at_once):
        self.buf, self.sems = buf, sems
        self.turns, size = buf.shape[0], at_once * ROWS
        self.parts = [[] for _ in range(self.turns)]
        first = 0
        for n, piece in enumerate(pieces):
            turn, row = divmod(first, size)
            self.parts[turn].append((n, row, piece.shape[0]))
            pltpu.make_async_copy(
                piece, buf.at[turn, pl.ds(row, piece.shape[0])], sems.at[n]
            ).start()
            first += piece.shape[0]

    def turn(self, n):
        def wait(parts, number):
            for i, (_, row, rows) in enumerate(parts):
                block = self.buf.at[n, pl.ds(row, rows)]
                pltpu.make_async_copy(block, block, self.sems.at[number + i]).wait()

        usual = len(self.parts[0])
        if len(self.parts[-1]) == usual:
            wait(self.parts[0], n * usual)
        else:

            @pl.when(n < self.turns - 1)
            def _():
                wait(self.parts[0], n * usual)

            @pl.when(n == self.turns - 1)
            def _():
                wait(self.parts[-1], (self.turns - 1) * usual)

        return self.buf.at[n]


def forward_kernel(pieces, at_once, first, last, number_ref, *refs):
    q_ref, refs = refs[0], refs[1:]
    chunks, refs = refs[:pieces], refs[pieces:]
    bias_ref, refs = refs[0], refs[1:]
    if not first:
        state_in, refs = refs[0], refs[1:]
    if last:
        g_ref, o_ref, stat_ref, state, buf, sems = refs
    else:
        state, buf, sems = refs
    blocks = Staged(chunks, buf, sems, at_once)
    if first:
        state[0] = jnp.full_like(state[0], NEG)
        state[1] = jnp.zeros_like(state[1])
        state[2] = jnp.zeros_like(state[2])
    else:
        state[...] = state_in[...]

    @pl.loop(0, blocks.turns)
    def _(n):
        kv = blocks.turn(n)
        s = dot_nt(q_ref[...], kv[:, :HD]) * C2
        s = with_bias(s, bias_ref, [number_ref[n * at_once + i] * 8 for i in range(at_once)])
        old = state[0]
        top = functools.reduce(jnp.maximum, tiles(s))
        new = jnp.maximum(old, jnp.max(top, axis=1, keepdims=True))
        fade = jnp.exp2(old - new)
        e = jnp.exp2(s - wide(new, at_once))
        state[0] = new
        state[1] = state[1] * fade + sum(tiles(e))
        state[2] = state[2] * fade + dot(e.astype(BF), kv[:, HD:])

    if last:
        total = jnp.sum(state[1], axis=1, keepdims=True)
        combined = state[2] * (1.0 / total)
        o_ref[...] = combined.astype(BF)
        lse = state[0] + jnp.log2(total)
        delta = jnp.sum(combined * g_ref[...].astype(F32), axis=1, keepdims=True)
        delta = jnp.broadcast_to(delta, (ROWS, HD))
        stat_ref[0:1, :] = lse.T[0:1, :]
        stat_ref[1:2, :] = delta.T[0:1, :]


def backward_kernel(pieces, first, last, q_ref, g_ref, stat_ref, number_ref, *refs):
    chunks, refs = refs[:pieces], refs[pieces:]
    bias_ref, refs = refs[0], refs[1:]
    if not first:
        acc_in, refs = refs[0], refs[1:]
    part_ref, refs = refs[0], refs[1:]
    if last:
        dq_ref, acc, buf, sems = refs
    else:
        acc, buf, sems = refs
    blocks = Staged(chunks, buf, sems, 1)
    if first:
        acc[...] = jnp.zeros_like(acc)
    else:
        acc[...] = acc_in[...]

    @pl.loop(0, blocks.turns)
    def _(n):
        kv = blocks.turn(n)
        q = q_ref[...]
        g = g_ref[...]
        k = kv[:, :HD]
        s = dot_nt(k, q) * C2
        p = jnp.exp2(with_bias(s, bias_ref, [number_ref[n] * 8]) - stat_ref[0:1, :])
        dp = dot_nt(kv[:, HD:], g)
        ds = (p * (dp - stat_ref[1:2, :])).astype(BF)
        part_ref[n, :, :HD] = (dot(ds, q) * SCALE).astype(BF)
        part_ref[n, :, HD:] = dot(p.astype(BF), g).astype(BF)
        acc[...] += dot(k.T, ds)

    if last:
        dq_ref[...] = (acc[...] * SCALE).T.astype(BF)


def bring(blocks, buf, sems):
    size = blocks[0].shape[0]
    copies = [
        pltpu.make_async_copy(block, buf.at[pl.ds(d * size, size)], sems.at[d])
        for d, block in enumerate(blocks)
    ]
    for copy in copies:
        copy.start()
    return [copy.wait for copy in copies]


def tokens_kernel(*refs):
    blocks, (w_ref, kv_ref, q_ref, x_ref) = refs[:HEADS], refs[HEADS:]
    for d, block in enumerate(blocks):
        rows = pl.ds(d * block.shape[0], block.shape[0])
        x_ref[rows, :] = block[...]
        kvq = dot(block[...], w_ref[...]).astype(BF)
        kv_ref[rows, :] = kvq[:, : 2 * HD]
        q_ref[rows, :] = kvq[:, 2 * HD :]


def cotangent_kernel(f_ref, a_ref, b_ref, *refs):
    blocks, (g_ref, dy_ref, out_ref) = refs[:HEADS], refs[HEADS:]
    size = a_ref.shape[0]
    turned = f_ref[0] // (NF // 2) * size
    out_ref[pl.ds(pl.multiple_of(turned, size), size), :] = a_ref[...]
    out_ref[pl.ds(pl.multiple_of(size - turned, size), size), :] = b_ref[...]
    for d, block in enumerate(blocks):
        rows = pl.ds(d * block.shape[0], block.shape[0])
        dy_ref[rows, :] = block[...]
        g_ref[rows, :] = dot_nt(block[...], out_ref[...]).astype(BF)


def out_kernel(h_ref, *refs):
    blocks, (dy_ref, o_ref, att, dy, sems, sem) = refs[:HEADS], refs[HEADS:]
    h = h_ref[0]
    part = dy_ref.at[:, pl.ds(pl.multiple_of(h * 256, 256), 256)]
    copy = pltpu.make_async_copy(part, dy, sem)
    copy.start()
    waits = bring(blocks, att, sems)
    copy.wait()
    size = ROWS // HEADS
    for d, wait in enumerate(waits):
        wait()
        rows = jnp.concatenate(
            [att[d * ROWS + (i ^ d) * size : d * ROWS + (i ^ d) * size + size, :] for i in range(HEADS)],
            axis=0,
        )
        grad = dot_tn(rows, dy[...]).astype(BF)
        for e in range(2):
            for c in range(2):
                o_ref[2 * (h ^ d) + e, c * 64 : (c + 1) * 64, :] = grad[
                    e * 64 : (e + 1) * 64, c * HD : (c + 1) * HD
                ]


def heads_kernel(transposed, a_ref, w_ref, own_ref, send_ref):
    terms = (dot_nt if transposed else dot)(a_ref[...], w_ref[...])
    size = ROWS // HEADS
    for i in range(2):
        own_ref[i] = terms[2 * i * size : (2 * i + 1) * size]
        send_ref[i] = terms[(2 * i + 1) * size : (2 * i + 2) * size].astype(BF)


def chip_kernel(own_ref, got_ref, keep_ref, send_ref):
    keep_ref[...] = own_ref[0] + got_ref[0].astype(F32)
    send_ref[...] = (own_ref[1] + got_ref[1].astype(F32)).astype(BF)


def call(kernel, name, out_shape, scratch, flops, *args, there=()):
    many = isinstance(out_shape, tuple)
    vmem = pl.BlockSpec(memory_space=pltpu.VMEM)
    smem = pl.BlockSpec(memory_space=pltpu.SMEM)
    specs = [smem if a.dtype == jnp.int32 else vmem for a in args]
    for n in there:
        specs[n] = pl.BlockSpec(memory_space=pltpu.MemorySpace.HBM)
    return pl.pallas_call(
        kernel,
        name=name,
        out_shape=out_shape,
        in_specs=specs,
        out_specs=(vmem,) * len(out_shape) if many else vmem,
        scratch_shapes=scratch,
        compiler_params=pltpu.CompilerParams(vmem_limit_bytes=VMEM_LIMIT),
        cost_estimate=pl.CostEstimate(
            flops=flops, bytes_accessed=1 << 20, transcendentals=flops // 2560
        ),
    )(*args)


def take(x, axis, size, by):
    return lax.ppermute(x, axis, [((i + by) % size, i) for i in range(size)])


def swap(x, bit):
    return lax.ppermute(x, "h", [(i, i ^ bit) for i in range(HEADS)])


def gather(x):
    far = swap(x, 2)
    return [x, swap(x, 1), far, swap(far, 1)]


def after(x, *others):
    return lax.optimization_barrier((x,) + others)[0]


def heads_terms(a, w, transposed):
    size = ROWS // HEADS
    own, send = call(
        functools.partial(heads_kernel, transposed),
        "heads_terms",
        (jax.ShapeDtypeStruct((2, size, 1024), F32), jax.ShapeDtypeStruct((2, size, 1024), BF)),
        [],
        2 * FLOPS * ROWS * 1024 * a.shape[1],
        a,
        w,
    )
    return own, swap(send, 1)


def add_heads(own, got, *others):
    size = ROWS // HEADS
    keep, send = call(
        chip_kernel,
        "heads_sum",
        (jax.ShapeDtypeStruct((size, 1024), F32), jax.ShapeDtypeStruct((size, 1024), BF)),
        [],
        10**8,
        own,
        got,
    )
    return keep + swap(after(send, *others), 2).astype(F32)


def exchange(x, axis):
    return lax.all_to_all(x, axis, split_axis=0, concat_axis=0, tiled=True)


class Ring:
    def __init__(self, block):
        self.blocks = {0: [block]}
        self.steps = 0

    def step(self, *others):
        r = self.steps = self.steps + 1
        up, down = self.blocks[r - 1][0], self.blocks[(1 - r) % NZ][0]
        if r < NZ // 2:
            self.blocks[r] = [take(after(up, *others), "z", NZ, 1)]
            self.blocks[NZ - r] = [take(after(down, *others), "z", NZ, -1)]
        else:
            half = ROWS // 2
            self.blocks[r] = [
                take(after(up[:half], *others), "z", NZ, 1),
                take(after(down[half:], *others), "z", NZ, -1),
            ]

    def pieces(self, number):
        return [piece for d in number for piece in self.blocks[d]]


def spread(x, axis, size):
    return exchange(jnp.broadcast_to(x[None], (size,) + x.shape), axis)


def span_bias(block_mask, span_order, z, h):
    order = jnp.tile(span_order.reshape(NZ, 2, 2, 2), (2, 1, 1, 1))
    order = lax.dynamic_slice(order, (z, 0, 0, 0), (NZ, 2, 2, 2))
    order = jnp.where(h // 2 == 1, order[:, ::-1], order)
    order = jnp.where(h % 2 == 1, order[:, :, ::-1], order).reshape(64) // 2
    hot = (order[:, None] == jnp.arange(32, dtype=jnp.int32)[None, :]).astype(F32)
    linked = dot(dot(hot, block_mask.astype(F32)), hot.T)
    bias = jnp.where(linked > 0.5, 0.0, NEG).astype(F32)
    by_group = jnp.transpose(bias[:8].reshape(8, NZ, 8), (1, 0, 2)).reshape(64, 8)
    both = jnp.repeat(jnp.concatenate([by_group, bias[:8].T]), SPAN, axis=1)
    return both[:64, None, :], both[64:, None, :]


def body(tokens, cotangent, w_query, w_key, w_value, w_out, block_mask, span_order):
    x_own = tokens[0]
    dy_own = cotangent[0]
    h = lax.axis_index("h")
    z = lax.axis_index("z")
    bias_q, bias_b = span_bias(block_mask, span_order, z, h)

    def head(w):
        return lax.dynamic_slice(w, (0, h * HD), (w.shape[0], HD))

    work = FLOPS * ROWS * ROWS * HD
    head_rows = jax.ShapeDtypeStruct((ROWS, HD), BF)
    pair_rows = jax.ShapeDtypeStruct((ROWS, 2 * HD), BF)
    model_rows = jax.ShapeDtypeStruct((ROWS, 1024), BF)
    state_shape = (3, ROWS, HD)
    acc_shape = (HD, ROWS)

    def staging(groups, at_once, pieces):
        blocks = pltpu.VMEM((groups // at_once, at_once * ROWS, 2 * HD), BF)
        return [blocks, pltpu.SemaphoreType.DMA((pieces,))]

    x_near = gather(x_own)

    def half_of_head(turned):
        pairs = []
        for m in range(NF):
            for a in range(HEADS):
                clip = 2 * a + (m // 4) ^ turned
                pairs.append((clip * HEADS + m % 4, m * HEADS + a))
        return lax.ppermute(after(w_out, x_near[2]), ("f", "h"), pairs)

    halves = half_of_head(0), half_of_head(1)
    mine = jnp.concatenate([head(w_key), head(w_value), head(w_query)], axis=1)
    w_head = spread(mine, "f", NF).reshape(1024, 3 * HD)
    kv, q, x = call(
        tokens_kernel,
        "tokens",
        (pair_rows, head_rows, model_rows),
        [],
        3 * work,
        *x_near,
        after(w_head, bias_q, bias_b, *halves),
    )
    kv_ring = Ring(kv)
    kv_ring.step()
    dy_near = gather(after(dy_own, kv))
    g, dy, out_head = call(
        cotangent_kernel,
        "cotangent",
        (head_rows, model_rows, jax.ShapeDtypeStruct((HD, 1024), BF)),
        [],
        2 * work,
        lax.axis_index("f").reshape(1),
        *halves,
        *dy_near,
    )

    def forward(number, state, *more, q=q):
        at_once = 1
        pieces = kv_ring.pieces(number)
        last = bool(more)
        shape = jax.ShapeDtypeStruct(state_shape, F32)
        if last:
            shape = (
                head_rows,
                jax.ShapeDtypeStruct((2, ROWS), F32),
            )
        count = len(number)
        return call(
            functools.partial(forward_kernel, len(pieces), at_once, not state, last),
            "attn_forward_end" if last else "attn_forward",
            shape,
            ([pltpu.VMEM(state_shape, F32)] if last else []) + staging(count, at_once, len(pieces)),
            2 * work * count,
            jnp.array(number, jnp.int32),
            q,
            *pieces,
            bias_q,
            *state,
            *more,
            there=range(2, 2 + len(pieces)),
        )

    kv_ring.step()
    state = (forward((0, 1, 7), (), q=after(q, *dy_near)),)
    kv_ring.step(*state)
    state = (forward((2, 6), state),)
    kv_ring.step(*state)
    state = (forward((3, 5), state),)
    att, stat = forward((4,), state, g)

    def backward(number, acc, last=False):
        pieces = kv_ring.pieces(number)
        count = len(number)
        out = call(
            functools.partial(backward_kernel, len(pieces), not acc, last),
            "attn_backward",
            (
                jax.ShapeDtypeStruct((count, ROWS, 2 * HD), BF),
                head_rows if last else jax.ShapeDtypeStruct(acc_shape, F32),
            ),
            ([pltpu.VMEM(acc_shape, F32)] if last else []) + staging(count, 1, len(pieces)),
            5 * work * count,
            q,
            g,
            stat,
            jnp.array(number, jnp.int32),
            *pieces,
            bias_b,
            *acc,
            there=range(4, 4 + len(pieces)),
        )
        return out

    def add(part, got):
        return (part.astype(F32) + got.astype(F32)).astype(BF)

    half = ROWS // 2
    part, acc = backward((4,), ())
    up = take(part[0, :half], "z", NZ, -1)
    down = take(part[0, half:], "z", NZ, 1)
    part, acc = backward((3, 5), (acc,))
    up = jnp.concatenate([add(part[0, :half], up), part[0, half:]], axis=0)
    down = jnp.concatenate([part[1, :half], add(part[1, half:], down)], axis=0)
    up, down = take(up, "z", NZ, -1), take(down, "z", NZ, 1)
    mixed = heads_terms(after(att, acc), out_head, False)
    part, acc = backward((2, 6), (acc,))
    up, down = add(part[0], up), add(part[1], down)
    part, dq = backward((1, 7, 0), (after(acc, up, down),), last=True)
    up, down = take(up, "z", NZ, -1), take(down, "z", NZ, 1)
    up, down = add(part[0], up), add(part[1], down)
    up, down = take(up, "z", NZ, -1), take(down, "z", NZ, 1)

    mixed = (x_own.astype(F32) + add_heads(*mixed)).astype(BF)
    grad_o = call(
        out_kernel,
        "grad_out",
        jax.ShapeDtypeStruct((NF, HD, HD), BF),
        [
            pltpu.VMEM((HEADS * ROWS, HD), BF),
            pltpu.VMEM((ROWS, 256), BF),
            pltpu.SemaphoreType.DMA((HEADS,)),
            pltpu.SemaphoreType.DMA,
        ],
        2 * work,
        h.reshape(1),
        *gather(att),
        dy,
        there=range(1, HEADS + 2),
    )
    grad_q = dot_tn(x, dq).astype(BF).reshape(NF, HD, HD)

    own = after(part[2], grad_q, grad_o, mixed)
    dkv = (own.astype(F32) + up.astype(F32) + down.astype(F32)).astype(BF)

    grad_kv = dot_tn(x, dkv).astype(BF).reshape(NF, HD, 2 * HD)
    terms = jnp.concatenate([grad_q, grad_kv, grad_o], axis=2)
    got = jnp.sum(exchange(terms, "f").astype(F32), axis=0).astype(BF)
    got_o = jnp.transpose(got[:, 3 * HD :].reshape(2, 32, 2, HD), (1, 0, 2, 3)).reshape(32, 4, HD)
    got = jnp.concatenate([got[:, : 3 * HD].reshape(32, 4, 3 * HD), got_o], axis=2)
    d_head = jnp.concatenate([after(dkv, terms), dq], axis=1)
    token_grad = heads_terms(d_head, w_head, True)
    token_grad = (dy_own.astype(F32) + add_heads(*token_grad, got)).astype(BF)

    sums = after(exchange(got, ("z", "h")), token_grad).reshape(NZ, HEADS, 4, 4 * HD)
    sums = jnp.sum(sums.astype(F32), axis=0)
    grads = sums[:, :, : 3 * HD].reshape(HEADS, 4, 3, HD)
    grads = jnp.transpose(grads, (2, 1, 0, 3)).reshape(3, 4, HEADS * HD)
    grad_o = sums[:, :, 3 * HD :].reshape(HEADS, 2, 2, HD)
    grad_o = jnp.transpose(grad_o, (2, 0, 1, 3)).reshape(2, 1024)
    return (mixed[None], token_grad[None], grads[0], grads[1], grads[2], grad_o)


def solution(mesh):
    fine = Mesh(mesh.devices.reshape(NF, NZ, HEADS), ("f", "z", "h"))
    rows = P("f", ("z", "h"), None)
    split = P(("f", "z", "h"), None)
    return jax.shard_map(
        body,
        mesh=fine,
        in_specs=(rows, rows, P("f", None), P("f", None), P("f", None), P("f", None), P(), P()),
        out_specs=(rows, rows, split, split, split, split),
        check_vma=False,
    )
```

```python
import functools
import math

import jax
import jax.numpy as jnp
from jax import lax
from jax.experimental import pallas as pl
from jax.experimental.pallas import tpu as pltpu
from jax.sharding import Mesh
from jax.sharding import PartitionSpec as P

HEADS = 4
HD = 128
SPAN = 64
NF = 8
NZ = 8
ROWS = 512
NEG = -1e30
SCALE = 1.0 / math.sqrt(HD)
C2 = SCALE * math.log2(math.e)
FLOPS = 8
VMEM_LIMIT = 16 << 20
BF = jnp.bfloat16
F32 = jnp.float32


def dot(a, b):
    return jnp.dot(a, b, preferred_element_type=F32)


def dot_nt(a, b):
    return lax.dot_general(a, b, (((1,), (1,)), ((), ())), preferred_element_type=F32)


def dot_tn(a, b):
    return lax.dot_general(a, b, (((0,), (0,)), ((), ())), preferred_element_type=F32)


def with_bias(s, bias_ref, firsts):
    parts = []
    for t in range(ROWS // SPAN):
        row = jnp.concatenate([bias_ref[first + t] for first in firsts], axis=1)
        parts.append(s[t * SPAN : (t + 1) * SPAN, :] + row)
    return jnp.concatenate(parts, axis=0)


def tiles(s):
    return [s[:, t * HD : (t + 1) * HD] for t in range(s.shape[1] // HD)]


def wide(row, count):
    return jnp.concatenate([row] * (count * (ROWS // HD)), axis=1)


class Staged:
    def __init__(self, pieces, buf, sems, at_once):
        self.buf, self.sems = buf, sems
        self.turns, size = buf.shape[0], at_once * ROWS
        self.parts = [[] for _ in range(self.turns)]
        first = 0
        for n, piece in enumerate(pieces):
            turn, row = divmod(first, size)
            self.parts[turn].append((n, row, piece.shape[0]))
            pltpu.make_async_copy(
                piece, buf.at[turn, pl.ds(row, piece.shape[0])], sems.at[n]
            ).start()
            first += piece.shape[0]

    def turn(self, n):
        def wait(parts, number):
            for i, (_, row, rows) in enumerate(parts):
                block = self.buf.at[n, pl.ds(row, rows)]
                pltpu.make_async_copy(block, block, self.sems.at[number + i]).wait()

        usual = len(self.parts[0])
        if len(self.parts[-1]) == usual:
            wait(self.parts[0], n * usual)
        else:

            @pl.when(n < self.turns - 1)
            def _():
                wait(self.parts[0], n * usual)

            @pl.when(n == self.turns - 1)
            def _():
                wait(self.parts[-1], (self.turns - 1) * usual)

        return self.buf.at[n]


def forward_kernel(pieces, at_once, first, last, number_ref, *refs):
    q_ref, refs = refs[0], refs[1:]
    chunks, refs = refs[:pieces], refs[pieces:]
    bias_ref, refs = refs[0], refs[1:]
    if not first:
        state_in, refs = refs[0], refs[1:]
    if last:
        g_ref, o_ref, stat_ref, state, buf, sems = refs
    else:
        state, buf, sems = refs
    blocks = Staged(chunks, buf, sems, at_once)
    if first:
        state[0] = jnp.full_like(state[0], NEG)
        state[1] = jnp.zeros_like(state[1])
        state[2] = jnp.zeros_like(state[2])
    else:
        state[...] = state_in[...]

    @pl.loop(0, blocks.turns)
    def _(n):
        kv = blocks.turn(n)
        s = dot_nt(q_ref[...], kv[:, :HD]) * C2
        s = with_bias(s, bias_ref, [number_ref[n * at_once + i] * 8 for i in range(at_once)])
        old = state[0]
        top = functools.reduce(jnp.maximum, tiles(s))
        new = jnp.maximum(old, jnp.max(top, axis=1, keepdims=True))
        fade = jnp.exp2(old - new)
        e = jnp.exp2(s - wide(new, at_once))
        state[0] = new
        state[1] = state[1] * fade + sum(tiles(e))
        state[2] = state[2] * fade + dot(e.astype(BF), kv[:, HD:])

    if last:
        total = jnp.sum(state[1], axis=1, keepdims=True)
        combined = state[2] * (1.0 / total)
        o_ref[...] = combined.astype(BF)
        lse = state[0] + jnp.log2(total)
        delta = jnp.sum(combined * g_ref[...].astype(F32), axis=1, keepdims=True)
        delta = jnp.broadcast_to(delta, (ROWS, HD))
        stat_ref[0:1, :] = lse.T[0:1, :]
        stat_ref[1:2, :] = delta.T[0:1, :]


def backward_kernel(pieces, first, last, q_ref, g_ref, stat_ref, number_ref, *refs):
    chunks, refs = refs[:pieces], refs[pieces:]
    bias_ref, refs = refs[0], refs[1:]
    if not first:
        acc_in, refs = refs[0], refs[1:]
    part_ref, refs = refs[0], refs[1:]
    if last:
        dq_ref, acc, buf, sems = refs
    else:
        acc, buf, sems = refs
    blocks = Staged(chunks, buf, sems, 1)
    if first:
        acc[...] = jnp.zeros_like(acc)
    else:
        acc[...] = acc_in[...]

    @pl.loop(0, blocks.turns)
    def _(n):
        kv = blocks.turn(n)
        q = q_ref[...]
        g = g_ref[...]
        k = kv[:, :HD]
        s = dot_nt(k, q) * C2
        p = jnp.exp2(with_bias(s, bias_ref, [number_ref[n] * 8]) - stat_ref[0:1, :])
        dp = dot_nt(kv[:, HD:], g)
        ds = (p * (dp - stat_ref[1:2, :])).astype(BF)
        part_ref[n, :, :HD] = (dot(ds, q) * SCALE).astype(BF)
        part_ref[n, :, HD:] = dot(p.astype(BF), g).astype(BF)
        acc[...] += dot(k.T, ds)

    if last:
        dq_ref[...] = (acc[...] * SCALE).T.astype(BF)


def bring(blocks, buf, sems):
    size = blocks[0].shape[0]
    copies = [
        pltpu.make_async_copy(block, buf.at[pl.ds(d * size, size)], sems.at[d])
        for d, block in enumerate(blocks)
    ]
    for copy in copies:
        copy.start()
    return [copy.wait for copy in copies]


def rows_kernel(*refs):
    blocks, (x_ref,) = refs[:HEADS], refs[HEADS:]
    for d, block in enumerate(blocks):
        x_ref[pl.ds(d * block.shape[0], block.shape[0]), :] = block[...]


def tokens_kernel(x_ref, w_ref, kv_ref, q_ref):
    kvq = dot(x_ref[...], w_ref[...]).astype(BF)
    kv_ref[...] = kvq[:, : 2 * HD]
    q_ref[...] = kvq[:, 2 * HD :]


def cotangent_kernel(f_ref, a_ref, b_ref, *refs):
    blocks, (g_ref, dy_ref, out_ref) = refs[:HEADS], refs[HEADS:]
    size = a_ref.shape[0]
    turned = f_ref[0] // (NF // 2) * size
    out_ref[pl.ds(pl.multiple_of(turned, size), size), :] = a_ref[...]
    out_ref[pl.ds(pl.multiple_of(size - turned, size), size), :] = b_ref[...]
    for d, block in enumerate(blocks):
        rows = pl.ds(d * block.shape[0], block.shape[0])
        dy_ref[rows, :] = block[...]
        g_ref[rows, :] = dot_nt(block[...], out_ref[...]).astype(BF)


def out_kernel(h_ref, *refs):
    blocks, (dy_ref, o_ref, att, dy, sems, sem) = refs[:HEADS], refs[HEADS:]
    h = h_ref[0]
    part = dy_ref.at[:, pl.ds(pl.multiple_of(h * 256, 256), 256)]
    copy = pltpu.make_async_copy(part, dy, sem)
    copy.start()
    waits = bring(blocks, att, sems)
    copy.wait()
    size = ROWS // HEADS
    for d, wait in enumerate(waits):
        wait()
        rows = jnp.concatenate(
            [att[d * ROWS + (i ^ d) * size : d * ROWS + (i ^ d) * size + size, :] for i in range(HEADS)],
            axis=0,
        )
        grad = dot_tn(rows, dy[...]).astype(BF)
        for e in range(2):
            for c in range(2):
                o_ref[2 * (h ^ d) + e, c * 64 : (c + 1) * 64, :] = grad[
                    e * 64 : (e + 1) * 64, c * HD : (c + 1) * HD
                ]


def clips_kernel(got_ref, out_ref):
    total = functools.reduce(jnp.add, [got_ref[f].astype(F32) for f in range(NF)])
    out_ref[:, :, : 3 * HD] = total[:, : 3 * HD].reshape(32, 4, 3 * HD).astype(BF)
    rows_o = total[:, 3 * HD :].reshape(64, 2, HD).astype(BF)
    out_ref[:, 0:2, 3 * HD :] = rows_o[:32]
    out_ref[:, 2:4, 3 * HD :] = rows_o[32:]


def heads_kernel(transposed, a_ref, w_ref, own_ref, send_ref):
    terms = (dot_nt if transposed else dot)(a_ref[...], w_ref[...])
    size = ROWS // HEADS
    for i in range(2):
        own_ref[i] = terms[2 * i * size : (2 * i + 1) * size]
        send_ref[i] = terms[(2 * i + 1) * size : (2 * i + 2) * size].astype(BF)


def chip_kernel(own_ref, got_ref, keep_ref, send_ref):
    keep_ref[...] = own_ref[0] + got_ref[0].astype(F32)
    send_ref[...] = (own_ref[1] + got_ref[1].astype(F32)).astype(BF)


def call(kernel, name, out_shape, scratch, flops, *args, there=()):
    many = isinstance(out_shape, tuple)
    vmem = pl.BlockSpec(memory_space=pltpu.VMEM)
    smem = pl.BlockSpec(memory_space=pltpu.SMEM)
    specs = [smem if a.dtype == jnp.int32 else vmem for a in args]
    for n in there:
        specs[n] = pl.BlockSpec(memory_space=pltpu.MemorySpace.HBM)
    return pl.pallas_call(
        kernel,
        name=name,
        out_shape=out_shape,
        in_specs=specs,
        out_specs=(vmem,) * len(out_shape) if many else vmem,
        scratch_shapes=scratch,
        compiler_params=pltpu.CompilerParams(vmem_limit_bytes=VMEM_LIMIT),
        cost_estimate=pl.CostEstimate(
            flops=flops, bytes_accessed=1 << 20, transcendentals=flops // 2560
        ),
    )(*args)


def take(x, axis, size, by):
    return lax.ppermute(x, axis, [((i + by) % size, i) for i in range(size)])


def swap(x, bit):
    return lax.ppermute(x, "h", [(i, i ^ bit) for i in range(HEADS)])


def gather(x):
    far = swap(x, 2)
    return [x, swap(x, 1), far, swap(far, 1)]


def after(x, *others):
    return lax.optimization_barrier((x,) + others)[0]


def heads_terms(a, w, transposed):
    size = ROWS // HEADS
    own, send = call(
        functools.partial(heads_kernel, transposed),
        "heads_terms",
        (jax.ShapeDtypeStruct((2, size, 1024), F32), jax.ShapeDtypeStruct((2, size, 1024), BF)),
        [],
        2 * FLOPS * ROWS * 1024 * a.shape[1],
        a,
        w,
    )
    return own, swap(send, 1)


def add_heads(own, got, *others):
    size = ROWS // HEADS
    keep, send = call(
        chip_kernel,
        "heads_sum",
        (jax.ShapeDtypeStruct((size, 1024), F32), jax.ShapeDtypeStruct((size, 1024), BF)),
        [],
        10**8,
        own,
        got,
    )
    return keep + swap(after(send, *others), 2).astype(F32)


def exchange(x, axis):
    return lax.all_to_all(x, axis, split_axis=0, concat_axis=0, tiled=True)


class Ring:
    def __init__(self, block):
        self.blocks = {0: [block]}
        self.steps = 0

    def step(self, *others):
        r = self.steps = self.steps + 1
        up, down = self.blocks[r - 1][0], self.blocks[(1 - r) % NZ][0]
        if r < NZ // 2:
            self.blocks[r] = [take(after(up, *others), "z", NZ, 1)]
            self.blocks[NZ - r] = [take(after(down, *others), "z", NZ, -1)]
        else:
            half = ROWS // 2
            self.blocks[r] = [
                take(after(up[:half], *others), "z", NZ, 1),
                take(after(down[half:], *others), "z", NZ, -1),
            ]

    def pieces(self, number):
        return [piece for d in number for piece in self.blocks[d]]


def spread(x, axis, size):
    return exchange(jnp.broadcast_to(x[None], (size,) + x.shape), axis)


def span_bias(block_mask, span_order, z, h):
    order = jnp.tile(span_order.reshape(NZ, 2, 2, 2), (2, 1, 1, 1))
    order = lax.dynamic_slice(order, (z, 0, 0, 0), (NZ, 2, 2, 2))
    order = jnp.where(h // 2 == 1, order[:, ::-1], order)
    order = jnp.where(h % 2 == 1, order[:, :, ::-1], order).reshape(64) // 2
    hot = (order[:, None] == jnp.arange(32, dtype=jnp.int32)[None, :]).astype(F32)
    linked = dot(dot(hot, block_mask.astype(F32)), hot.T)
    bias = jnp.where(linked > 0.5, 0.0, NEG).astype(F32)
    by_group = jnp.transpose(bias[:8].reshape(8, NZ, 8), (1, 0, 2)).reshape(64, 8)
    both = jnp.repeat(jnp.concatenate([by_group, bias[:8].T]), SPAN, axis=1)
    return both[:64, None, :], both[64:, None, :]


def body(tokens, cotangent, w_query, w_key, w_value, w_out, block_mask, span_order):
    x_own = tokens[0]
    dy_own = cotangent[0]
    h = lax.axis_index("h")
    z = lax.axis_index("z")
    bias_q, bias_b = span_bias(block_mask, span_order, z, h)

    def head(w):
        return lax.dynamic_slice(w, (0, h * HD), (w.shape[0], HD))

    work = FLOPS * ROWS * ROWS * HD
    head_rows = jax.ShapeDtypeStruct((ROWS, HD), BF)
    pair_rows = jax.ShapeDtypeStruct((ROWS, 2 * HD), BF)
    model_rows = jax.ShapeDtypeStruct((ROWS, 1024), BF)
    state_shape = (3, ROWS, HD)
    acc_shape = (HD, ROWS)

    def staging(groups, at_once, pieces):
        blocks = pltpu.VMEM((groups // at_once, at_once * ROWS, 2 * HD), BF)
        return [blocks, pltpu.SemaphoreType.DMA((pieces,))]

    x_near = gather(x_own)

    def half_of_head(turned):
        pairs = []
        for m in range(NF):
            for a in range(HEADS):
                clip = 2 * a + (m // 4) ^ turned
                pairs.append((clip * HEADS + m % 4, m * HEADS + a))
        return lax.ppermute(after(w_out, x_near[2]), ("f", "h"), pairs)

    halves = half_of_head(0), half_of_head(1)
    mine = jnp.concatenate([head(w_key), head(w_value), head(w_query)], axis=1)
    w_head = spread(mine, "f", NF).reshape(1024, 3 * HD)
    x = call(rows_kernel, "rows", model_rows, [], work // 4, *x_near)
    kv, q = call(
        tokens_kernel,
        "tokens",
        (pair_rows, head_rows),
        [],
        3 * work,
        x,
        after(w_head, x, bias_q, bias_b, *halves),
    )
    kv_ring = Ring(kv)
    kv_ring.step()
    def forward(number, state, *more, q=q):
        at_once = 1
        pieces = kv_ring.pieces(number)
        last = bool(more)
        shape = jax.ShapeDtypeStruct(state_shape, F32)
        if last:
            shape = (
                head_rows,
                jax.ShapeDtypeStruct((2, ROWS), F32),
            )
        count = len(number)
        return call(
            functools.partial(forward_kernel, len(pieces), at_once, not state, last),
            "attn_forward_end" if last else "attn_forward",
            shape,
            ([pltpu.VMEM(state_shape, F32)] if last else []) + staging(count, at_once, len(pieces)),
            2 * work * count,
            jnp.array(number, jnp.int32),
            q,
            *pieces,
            bias_q,
            *state,
            *more,
            there=range(2, 2 + len(pieces)),
        )

    dy_near = gather(after(dy_own, *kv_ring.blocks[1], *kv_ring.blocks[7]))
    g, dy, out_head = call(
        cotangent_kernel,
        "cotangent",
        (head_rows, model_rows, jax.ShapeDtypeStruct((HD, 1024), BF)),
        [],
        2 * work,
        lax.axis_index("f").reshape(1),
        *halves,
        *dy_near,
    )
    kv_ring.step()
    state = (forward((0, 1, 7), ()),)
    kv_ring.step(*state)
    kv_ring.step()
    state = (forward((2, 6, 3, 5), state),)
    att, stat = forward((4,), state, g)

    def backward(number, acc, last=False):
        pieces = kv_ring.pieces(number)
        count = len(number)
        out = call(
            functools.partial(backward_kernel, len(pieces), not acc, last),
            "attn_backward",
            (
                jax.ShapeDtypeStruct((count, ROWS, 2 * HD), BF),
                head_rows if last else jax.ShapeDtypeStruct(acc_shape, F32),
            ),
            ([pltpu.VMEM(acc_shape, F32)] if last else []) + staging(count, 1, len(pieces)),
            5 * work * count,
            q,
            g,
            stat,
            jnp.array(number, jnp.int32),
            *pieces,
            bias_b,
            *acc,
            there=range(4, 4 + len(pieces)),
        )
        return out

    def add(part, got):
        return (part.astype(F32) + got.astype(F32)).astype(BF)

    half = ROWS // 2
    part, acc = backward((4,), ())
    up = take(part[0, :half], "z", NZ, -1)
    down = take(part[0, half:], "z", NZ, 1)
    part, acc = backward((3, 5), (acc,))
    sent = acc
    up = jnp.concatenate([add(part[0, :half], up), part[0, half:]], axis=0)
    down = jnp.concatenate([part[1, :half], add(part[1, half:], down)], axis=0)
    up, down = take(up, "z", NZ, -1), take(down, "z", NZ, 1)
    mixed = heads_terms(after(att, acc), out_head, False)
    part, acc = backward((2, 6), (acc,))
    up, down = add(part[0], up), add(part[1], down)
    part, dq = backward((1, 7, 0), (after(acc, up, down),), last=True)
    up, down = take(up, "z", NZ, -1), take(down, "z", NZ, 1)
    up, down = add(part[0], up), add(part[1], down)
    up, down = take(up, "z", NZ, -1), take(down, "z", NZ, 1)

    mixed = (x_own.astype(F32) + add_heads(*mixed)).astype(BF)
    grad_o = call(
        out_kernel,
        "grad_out",
        jax.ShapeDtypeStruct((NF, HD, HD), BF),
        [
            pltpu.VMEM((HEADS * ROWS, HD), BF),
            pltpu.VMEM((ROWS, 256), BF),
            pltpu.SemaphoreType.DMA((HEADS,)),
            pltpu.SemaphoreType.DMA,
        ],
        2 * work,
        h.reshape(1),
        *gather(after(att, sent)),
        dy,
        there=range(1, HEADS + 2),
    )
    grad_q = dot_tn(x, dq).astype(BF).reshape(NF, HD, HD)

    own = after(part[2], grad_q, grad_o, mixed)
    dkv = (own.astype(F32) + up.astype(F32) + down.astype(F32)).astype(BF)

    grad_kv = dot_tn(x, dkv).astype(BF).reshape(NF, HD, 2 * HD)
    terms = jnp.concatenate([grad_q, grad_kv, grad_o], axis=2)
    got = call(
        clips_kernel,
        "clips_sum",
        jax.ShapeDtypeStruct((32, 4, 4 * HD), BF),
        [],
        10**8,
        exchange(terms, "f"),
    )
    d_head = jnp.concatenate([after(dkv, terms), dq], axis=1)
    token_grad = heads_terms(d_head, w_head, True)
    token_grad = (dy_own.astype(F32) + add_heads(*token_grad)).astype(BF)

    sums = after(exchange(got, ("z", "h")), token_grad).reshape(NZ, HEADS, 4, 4 * HD)
    sums = jnp.sum(sums.astype(F32), axis=0)
    grads = sums[:, :, : 3 * HD].reshape(HEADS, 4, 3, HD)
    grads = jnp.transpose(grads, (2, 1, 0, 3)).reshape(3, 4, HEADS * HD)
    grad_o = sums[:, :, 3 * HD :].reshape(HEADS, 2, 2, HD)
    grad_o = jnp.transpose(grad_o, (2, 0, 1, 3)).reshape(2, 1024)
    return (mixed[None], token_grad[None], grads[0], grads[1], grads[2], grad_o)


def solution(mesh):
    fine = Mesh(mesh.devices.reshape(NF, NZ, HEADS), ("f", "z", "h"))
    rows = P("f", ("z", "h"), None)
    split = P(("f", "z", "h"), None)
    return jax.shard_map(
        body,
        mesh=fine,
        in_specs=(rows, rows, P("f", None), P("f", None), P("f", None), P("f", None), P(), P()),
        out_specs=(rows, rows, split, split, split, split),
        check_vma=False,
    )
```

```python
import functools
import math

import jax
import jax.numpy as jnp
from jax import lax
from jax.experimental import pallas as pl
from jax.experimental.pallas import tpu as pltpu
from jax.sharding import Mesh
from jax.sharding import PartitionSpec as P

HEADS = 4
HD = 128
SPAN = 64
NF = 8
NZ = 8
ROWS = 512
NEG = -1e30
SCALE = 1.0 / math.sqrt(HD)
C2 = SCALE * math.log2(math.e)
FLOPS = 8
VMEM_LIMIT = 16 << 20
BF = jnp.bfloat16
F32 = jnp.float32


def dot(a, b):
    return jnp.dot(a, b, preferred_element_type=F32)


def dot_nt(a, b):
    return lax.dot_general(a, b, (((1,), (1,)), ((), ())), preferred_element_type=F32)


def dot_tn(a, b):
    return lax.dot_general(a, b, (((0,), (0,)), ((), ())), preferred_element_type=F32)


def with_bias(s, bias_ref, firsts):
    parts = []
    for t in range(ROWS // SPAN):
        row = jnp.concatenate([bias_ref[first + t] for first in firsts], axis=1)
        parts.append(s[t * SPAN : (t + 1) * SPAN, :] + row)
    return jnp.concatenate(parts, axis=0)


def tiles(s):
    return [s[:, t * HD : (t + 1) * HD] for t in range(s.shape[1] // HD)]


def wide(row, count):
    return jnp.concatenate([row] * (count * (ROWS // HD)), axis=1)


class Staged:
    def __init__(self, pieces, buf, sems, at_once):
        self.buf, self.sems = buf, sems
        self.turns, size = buf.shape[0], at_once * ROWS
        self.parts = [[] for _ in range(self.turns)]
        first = 0
        for n, piece in enumerate(pieces):
            turn, row = divmod(first, size)
            self.parts[turn].append((n, row, piece.shape[0]))
            pltpu.make_async_copy(
                piece, buf.at[turn, pl.ds(row, piece.shape[0])], sems.at[n]
            ).start()
            first += piece.shape[0]

    def turn(self, n):
        def wait(parts, number):
            for i, (_, row, rows) in enumerate(parts):
                block = self.buf.at[n, pl.ds(row, rows)]
                pltpu.make_async_copy(block, block, self.sems.at[number + i]).wait()

        usual = len(self.parts[0])
        if len(self.parts[-1]) == usual:
            wait(self.parts[0], n * usual)
        else:

            @pl.when(n < self.turns - 1)
            def _():
                wait(self.parts[0], n * usual)

            @pl.when(n == self.turns - 1)
            def _():
                wait(self.parts[-1], (self.turns - 1) * usual)

        return self.buf.at[n]


def forward_kernel(pieces, at_once, first, last, number_ref, *refs):
    q_ref, refs = refs[0], refs[1:]
    chunks, refs = refs[:pieces], refs[pieces:]
    bias_ref, refs = refs[0], refs[1:]
    if not first:
        state_in, refs = refs[0], refs[1:]
    if last:
        g_ref, o_ref, stat_ref, state, buf, sems = refs
    else:
        state, buf, sems = refs
    blocks = Staged(chunks, buf, sems, at_once)
    if first:
        state[0] = jnp.full_like(state[0], NEG)
        state[1] = jnp.zeros_like(state[1])
        state[2] = jnp.zeros_like(state[2])
    else:
        state[...] = state_in[...]

    @pl.loop(0, blocks.turns)
    def _(n):
        kv = blocks.turn(n)
        s = dot_nt(q_ref[...], kv[:, :HD]) * C2
        s = with_bias(s, bias_ref, [number_ref[n * at_once + i] * 8 for i in range(at_once)])
        old = state[0]
        top = functools.reduce(jnp.maximum, tiles(s))
        new = jnp.maximum(old, jnp.max(top, axis=1, keepdims=True))
        fade = jnp.exp2(old - new)
        e = jnp.exp2(s - wide(new, at_once))
        state[0] = new
        state[1] = state[1] * fade + sum(tiles(e))
        state[2] = state[2] * fade + dot(e.astype(BF), kv[:, HD:])

    if last:
        total = jnp.sum(state[1], axis=1, keepdims=True)
        combined = state[2] * (1.0 / total)
        o_ref[...] = combined.astype(BF)
        lse = state[0] + jnp.log2(total)
        delta = jnp.sum(combined * g_ref[...].astype(F32), axis=1, keepdims=True)
        delta = jnp.broadcast_to(delta, (ROWS, HD))
        stat_ref[0:1, :] = lse.T[0:1, :]
        stat_ref[1:2, :] = delta.T[0:1, :]


def backward_kernel(pieces, first, last, q_ref, g_ref, stat_ref, number_ref, *refs):
    chunks, refs = refs[:pieces], refs[pieces:]
    bias_ref, refs = refs[0], refs[1:]
    if not first:
        acc_in, refs = refs[0], refs[1:]
    part_ref, refs = refs[0], refs[1:]
    if last:
        dq_ref, acc, buf, sems = refs
    else:
        acc, buf, sems = refs
    blocks = Staged(chunks, buf, sems, 1)
    if first:
        acc[...] = jnp.zeros_like(acc)
    else:
        acc[...] = acc_in[...]

    @pl.loop(0, blocks.turns)
    def _(n):
        kv = blocks.turn(n)
        q = q_ref[...]
        g = g_ref[...]
        k = kv[:, :HD]
        s = dot_nt(k, q) * C2
        p = jnp.exp2(with_bias(s, bias_ref, [number_ref[n] * 8]) - stat_ref[0:1, :])
        dp = dot_nt(kv[:, HD:], g)
        ds = (p * (dp - stat_ref[1:2, :])).astype(BF)
        part_ref[n, :, :HD] = (dot(ds, q) * SCALE).astype(BF)
        part_ref[n, :, HD:] = dot(p.astype(BF), g).astype(BF)
        acc[...] += dot(k.T, ds)

    if last:
        dq_ref[...] = (acc[...] * SCALE).T.astype(BF)


def bring(blocks, buf, sems):
    size = blocks[0].shape[0]
    copies = [
        pltpu.make_async_copy(block, buf.at[pl.ds(d * size, size)], sems.at[d])
        for d, block in enumerate(blocks)
    ]
    for copy in copies:
        copy.start()
    return [copy.wait for copy in copies]


def rows_kernel(*refs):
    blocks, (x_ref,) = refs[:HEADS], refs[HEADS:]
    for d, block in enumerate(blocks):
        x_ref[pl.ds(d * block.shape[0], block.shape[0]), :] = block[...]


def tokens_kernel(x_ref, w_ref, kv_ref, q_ref):
    kvq = dot(x_ref[...], w_ref[...]).astype(BF)
    kv_ref[...] = kvq[:, : 2 * HD]
    q_ref[...] = kvq[:, 2 * HD :]


def cotangent_kernel(f_ref, a_ref, b_ref, *refs):
    blocks, (g_ref, dy_ref, out_ref) = refs[:HEADS], refs[HEADS:]
    size = a_ref.shape[0]
    turned = f_ref[0] // (NF // 2) * size
    out_ref[pl.ds(pl.multiple_of(turned, size), size), :] = a_ref[...]
    out_ref[pl.ds(pl.multiple_of(size - turned, size), size), :] = b_ref[...]
    for d, block in enumerate(blocks):
        rows = pl.ds(d * block.shape[0], block.shape[0])
        dy_ref[rows, :] = block[...]
        g_ref[rows, :] = dot_nt(block[...], out_ref[...]).astype(BF)


def out_kernel(h_ref, *refs):
    blocks, (dy_ref, o_ref, att, dy, sems, sem) = refs[:HEADS], refs[HEADS:]
    h = h_ref[0]
    part = dy_ref.at[:, pl.ds(pl.multiple_of(h * 256, 256), 256)]
    copy = pltpu.make_async_copy(part, dy, sem)
    copy.start()
    waits = bring(blocks, att, sems)
    copy.wait()
    size = ROWS // HEADS
    for d, wait in enumerate(waits):
        wait()
        rows = jnp.concatenate(
            [att[d * ROWS + (i ^ d) * size : d * ROWS + (i ^ d) * size + size, :] for i in range(HEADS)],
            axis=0,
        )
        grad = dot_tn(rows, dy[...]).astype(BF)
        for e in range(2):
            for c in range(2):
                o_ref[2 * (h ^ d) + e, c * 64 : (c + 1) * 64, :] = grad[
                    e * 64 : (e + 1) * 64, c * HD : (c + 1) * HD
                ]


def clips_kernel(got_ref, out_ref):
    total = functools.reduce(jnp.add, [got_ref[f].astype(F32) for f in range(NF)])
    out_ref[:, :, : 3 * HD] = total[:, : 3 * HD].reshape(32, 4, 3 * HD).astype(BF)
    rows_o = total[:, 3 * HD :].reshape(64, 2, HD).astype(BF)
    out_ref[:, 0:2, 3 * HD :] = rows_o[:32]
    out_ref[:, 2:4, 3 * HD :] = rows_o[32:]


def heads_kernel(transposed, a_ref, w_ref, own_ref, send_ref):
    terms = (dot_nt if transposed else dot)(a_ref[...], w_ref[...])
    size = ROWS // HEADS
    for i in range(2):
        own_ref[i] = terms[2 * i * size : (2 * i + 1) * size]
        send_ref[i] = terms[(2 * i + 1) * size : (2 * i + 2) * size].astype(BF)


def chip_kernel(own_ref, got_ref, keep_ref, send_ref):
    keep_ref[...] = own_ref[0] + got_ref[0].astype(F32)
    send_ref[...] = (own_ref[1] + got_ref[1].astype(F32)).astype(BF)


def call(kernel, name, out_shape, scratch, flops, *args, there=()):
    many = isinstance(out_shape, tuple)
    vmem = pl.BlockSpec(memory_space=pltpu.VMEM)
    smem = pl.BlockSpec(memory_space=pltpu.SMEM)
    specs = [smem if a.dtype == jnp.int32 else vmem for a in args]
    for n in there:
        specs[n] = pl.BlockSpec(memory_space=pltpu.MemorySpace.HBM)
    return pl.pallas_call(
        kernel,
        name=name,
        out_shape=out_shape,
        in_specs=specs,
        out_specs=(vmem,) * len(out_shape) if many else vmem,
        scratch_shapes=scratch,
        compiler_params=pltpu.CompilerParams(vmem_limit_bytes=VMEM_LIMIT),
        cost_estimate=pl.CostEstimate(
            flops=flops, bytes_accessed=1 << 20, transcendentals=flops // 2560
        ),
    )(*args)


def take(x, axis, size, by):
    return lax.ppermute(x, axis, [((i + by) % size, i) for i in range(size)])


def swap(x, bit):
    return lax.ppermute(x, "h", [(i, i ^ bit) for i in range(HEADS)])


def gather(x):
    far = swap(x, 2)
    return [x, swap(x, 1), far, swap(far, 1)]


def after(x, *others):
    return lax.optimization_barrier((x,) + others)[0]


def heads_terms(a, w, transposed):
    size = ROWS // HEADS
    own, send = call(
        functools.partial(heads_kernel, transposed),
        "heads_terms",
        (jax.ShapeDtypeStruct((2, size, 1024), F32), jax.ShapeDtypeStruct((2, size, 1024), BF)),
        [],
        2 * FLOPS * ROWS * 1024 * a.shape[1],
        a,
        w,
    )
    return own, swap(send, 1)


def add_heads(own, got, *others):
    size = ROWS // HEADS
    keep, send = call(
        chip_kernel,
        "heads_sum",
        (jax.ShapeDtypeStruct((size, 1024), F32), jax.ShapeDtypeStruct((size, 1024), BF)),
        [],
        10**8,
        own,
        got,
    )
    return keep + swap(after(send, *others), 2).astype(F32)


def exchange(x, axis):
    return lax.all_to_all(x, axis, split_axis=0, concat_axis=0, tiled=True)


class Ring:
    def __init__(self, block):
        self.blocks = {0: [block]}
        self.steps = 0

    def step(self, *others):
        r = self.steps = self.steps + 1
        up, down = self.blocks[r - 1][0], self.blocks[(1 - r) % NZ][0]
        if r < NZ // 2:
            self.blocks[r] = [take(after(up, *others), "z", NZ, 1)]
            self.blocks[NZ - r] = [take(after(down, *others), "z", NZ, -1)]
        else:
            half = ROWS // 2
            self.blocks[r] = [
                take(after(up[:half], *others), "z", NZ, 1),
                take(after(down[half:], *others), "z", NZ, -1),
            ]

    def pieces(self, number):
        return [piece for d in number for piece in self.blocks[d]]


def spread(x, axis, size):
    return exchange(jnp.broadcast_to(x[None], (size,) + x.shape), axis)


def span_bias(block_mask, span_order, z, h):
    order = jnp.tile(span_order.reshape(NZ, 2, 2, 2), (2, 1, 1, 1))
    order = lax.dynamic_slice(order, (z, 0, 0, 0), (NZ, 2, 2, 2))
    order = jnp.where(h // 2 == 1, order[:, ::-1], order)
    order = jnp.where(h % 2 == 1, order[:, :, ::-1], order).reshape(64) // 2
    hot = (order[:, None] == jnp.arange(32, dtype=jnp.int32)[None, :]).astype(F32)
    linked = dot(dot(hot, block_mask.astype(F32)), hot.T)
    bias = jnp.where(linked > 0.5, 0.0, NEG).astype(F32)
    by_group = jnp.transpose(bias[:8].reshape(8, NZ, 8), (1, 0, 2)).reshape(64, 8)
    both = jnp.repeat(jnp.concatenate([by_group, bias[:8].T]), SPAN, axis=1)
    return both[:64, None, :], both[64:, None, :]


def body(tokens, cotangent, w_query, w_key, w_value, w_out, block_mask, span_order):
    x_own = tokens[0]
    dy_own = cotangent[0]
    h = lax.axis_index("h")
    z = lax.axis_index("z")
    bias_q, bias_b = span_bias(block_mask, span_order, z, h)

    def head(w):
        return lax.dynamic_slice(w, (0, h * HD), (w.shape[0], HD))

    work = FLOPS * ROWS * ROWS * HD
    head_rows = jax.ShapeDtypeStruct((ROWS, HD), BF)
    pair_rows = jax.ShapeDtypeStruct((ROWS, 2 * HD), BF)
    model_rows = jax.ShapeDtypeStruct((ROWS, 1024), BF)
    state_shape = (3, ROWS, HD)
    acc_shape = (HD, ROWS)

    def staging(groups, at_once, pieces):
        blocks = pltpu.VMEM((groups // at_once, at_once * ROWS, 2 * HD), BF)
        return [blocks, pltpu.SemaphoreType.DMA((pieces,))]

    x_near = gather(x_own)

    def half_of_head(turned):
        pairs = []
        for m in range(NF):
            for a in range(HEADS):
                clip = 2 * a + (m // 4) ^ turned
                pairs.append((clip * HEADS + m % 4, m * HEADS + a))
        return lax.ppermute(after(w_out, x_near[2]), ("f", "h"), pairs)

    halves = half_of_head(0), half_of_head(1)
    mine = jnp.concatenate([head(w_key), head(w_value), head(w_query)], axis=1)
    w_head = spread(mine, "f", NF).reshape(1024, 3 * HD)
    x = call(rows_kernel, "rows", model_rows, [], work // 4, *x_near)
    kv, q = call(
        tokens_kernel,
        "tokens",
        (pair_rows, head_rows),
        [],
        3 * work,
        x,
        after(w_head, x, bias_q, bias_b, *halves),
    )
    kv_ring = Ring(kv)
    kv_ring.step()
    dy_near = gather(after(dy_own, kv))
    g, dy, out_head = call(
        cotangent_kernel,
        "cotangent",
        (head_rows, model_rows, jax.ShapeDtypeStruct((HD, 1024), BF)),
        [],
        2 * work,
        lax.axis_index("f").reshape(1),
        *halves,
        *dy_near,
    )

    def forward(number, state, *more, q=q):
        at_once = 1
        pieces = kv_ring.pieces(number)
        last = bool(more)
        shape = jax.ShapeDtypeStruct(state_shape, F32)
        if last:
            shape = (
                head_rows,
                jax.ShapeDtypeStruct((2, ROWS), F32),
            )
        count = len(number)
        return call(
            functools.partial(forward_kernel, len(pieces), at_once, not state, last),
            "attn_forward_end" if last else "attn_forward",
            shape,
            ([pltpu.VMEM(state_shape, F32)] if last else []) + staging(count, at_once, len(pieces)),
            2 * work * count,
            jnp.array(number, jnp.int32),
            q,
            *pieces,
            bias_q,
            *state,
            *more,
            there=range(2, 2 + len(pieces)),
        )

    kv_ring.step()
    state = (forward((0, 1, 7), (), q=after(q, *dy_near)),)
    kv_ring.step(*state)
    kv_ring.step()
    state = (forward((2, 6, 3, 5), state),)
    att, stat = forward((4,), state, g)

    def backward(number, acc, last=False):
        pieces = kv_ring.pieces(number)
        count = len(number)
        out = call(
            functools.partial(backward_kernel, len(pieces), not acc, last),
            "attn_backward",
            (
                jax.ShapeDtypeStruct((count, ROWS, 2 * HD), BF),
                head_rows if last else jax.ShapeDtypeStruct(acc_shape, F32),
            ),
            ([pltpu.VMEM(acc_shape, F32)] if last else []) + staging(count, 1, len(pieces)),
            5 * work * count,
            q,
            g,
            stat,
            jnp.array(number, jnp.int32),
            *pieces,
            bias_b,
            *acc,
            there=range(4, 4 + len(pieces)),
        )
        return out

    def add(part, got):
        return (part.astype(F32) + got.astype(F32)).astype(BF)

    half = ROWS // 2
    part, acc = backward((4,), ())
    up = take(part[0, :half], "z", NZ, -1)
    down = take(part[0, half:], "z", NZ, 1)
    part, acc = backward((3, 5), (acc,))
    up = jnp.concatenate([add(part[0, :half], up), part[0, half:]], axis=0)
    down = jnp.concatenate([part[1, :half], add(part[1, half:], down)], axis=0)
    up, down = take(up, "z", NZ, -1), take(down, "z", NZ, 1)
    mixed = heads_terms(after(att, acc), out_head, False)
    part, acc = backward((2, 6), (acc,))
    up, down = add(part[0], up), add(part[1], down)
    part, dq = backward((1, 7, 0), (after(acc, up, down),), last=True)
    up, down = take(up, "z", NZ, -1), take(down, "z", NZ, 1)
    up, down = add(part[0], up), add(part[1], down)
    up, down = take(up, "z", NZ, -1), take(down, "z", NZ, 1)

    mixed = (x_own.astype(F32) + add_heads(*mixed)).astype(BF)
    grad_o = call(
        out_kernel,
        "grad_out",
        jax.ShapeDtypeStruct((NF, HD, HD), BF),
        [
            pltpu.VMEM((HEADS * ROWS, HD), BF),
            pltpu.VMEM((ROWS, 256), BF),
            pltpu.SemaphoreType.DMA((HEADS,)),
            pltpu.SemaphoreType.DMA,
        ],
        2 * work,
        h.reshape(1),
        *gather(att),
        dy,
        there=range(1, HEADS + 2),
    )
    grad_q = dot_tn(x, dq).astype(BF).reshape(NF, HD, HD)

    own = after(part[2], grad_q, grad_o, mixed)
    dkv = (own.astype(F32) + up.astype(F32) + down.astype(F32)).astype(BF)

    grad_kv = dot_tn(x, dkv).astype(BF).reshape(NF, HD, 2 * HD)
    terms = jnp.concatenate([grad_q, grad_kv, grad_o], axis=2)
    got = call(
        clips_kernel,
        "clips_sum",
        jax.ShapeDtypeStruct((32, 4, 4 * HD), BF),
        [],
        10**8,
        exchange(terms, "f"),
    )
    d_head = jnp.concatenate([after(dkv, terms), dq], axis=1)
    token_grad = heads_terms(d_head, w_head, True)
    token_grad = (dy_own.astype(F32) + add_heads(*token_grad, got)).astype(BF)

    sums = after(exchange(got, ("z", "h")), token_grad).reshape(NZ, HEADS, 4, 4 * HD)
    sums = jnp.sum(sums.astype(F32), axis=0)
    grads = sums[:, :, : 3 * HD].reshape(HEADS, 4, 3, HD)
    grads = jnp.transpose(grads, (2, 1, 0, 3)).reshape(3, 4, HEADS * HD)
    grad_o = sums[:, :, 3 * HD :].reshape(HEADS, 2, 2, HD)
    grad_o = jnp.transpose(grad_o, (2, 0, 1, 3)).reshape(2, 1024)
    return (mixed[None], token_grad[None], grads[0], grads[1], grads[2], grad_o)


def solution(mesh):
    fine = Mesh(mesh.devices.reshape(NF, NZ, HEADS), ("f", "z", "h"))
    rows = P("f", ("z", "h"), None)
    split = P(("f", "z", "h"), None)
    return jax.shard_map(
        body,
        mesh=fine,
        in_specs=(rows, rows, P("f", None), P("f", None), P("f", None), P("f", None), P(), P()),
        out_specs=(rows, rows, split, split, split, split),
        check_vma=False,
    )
```
